512 devices in a mesh: dp: 4 (over y_lo, core), space: 128 (over z, x, y_hi).
Axes of the slice: x: 4, y: 8 (y_hi: 4, y_lo: 2; y = y_hi * 2 + y_lo), z: 8, core: 2. Of those that a mesh axis runs over, the one named last changes fastest.
Arguments:
- volume: bfloat16 [4, 256, 32, 48, 64], P('dp', 'space'), may hold values from -6 to 6
- cotangent: bfloat16 [4, 128, 16, 24, 256], P('dp', 'space'), may hold values from -6 to 6
- w_first: bfloat16 [3, 3, 3, 64, 128], replicated, may hold values from -0.15625 to 0.15625
- w_second: bfloat16 [3, 3, 3, 16, 256], replicated, may hold values from -0.3125 to 0.3125
Outputs:
- grad_input: bfloat16 [4, 256, 32, 48, 64], P('dp', 'space')
- grad_first: float32 [3, 3, 3, 64, 128], replicated
- grad_second: float32 [3, 3, 3, 16, 256], replicated
The draws below stay inside these ranges and needn't reach their ends.
All inputs are finite; a program needn't handle non-finite values.
Results may differ from the reference program's by a relative error of at most 0.0057.
Values may be sent and summed in bfloat16 or wider, within the bound.
No kernel may reach another device: no remote copies, remote signals or barrier semaphores. Data moves between devices by JAX's collectives and lax.ppermute only.
A program may use at most 64 MiB of HBM per device.

```python
import jax
import jax.numpy as jnp
from jax import lax

C1 = 64
CM = 128
CO = 256
GROUPS = 8
H = 32
W = 48
SAMPLES = 4
ND = 256
ND2 = 128
H2 = 16
W2 = 24
GIN = 16


def block_scale(stream_key, extent, pieces, low, top_value):
    level = 1.0
    for dim, parts in pieces:
        draws = jax.random.uniform(jax.random.fold_in(jax.random.fold_in(stream_key, 6), dim), (parts,), jnp.float32, low / len(pieces), top_value / len(pieces))
        level = level * jnp.repeat(jnp.exp(draws), extent[dim] // parts).reshape((-1,) + (1,) * (len(extent) - 1 - dim))
    return level


def bell_draw(rng, dims, spread, limit, cuts=(), held_as=jnp.bfloat16):
    entries = jax.random.normal(rng, dims, jnp.float32) * spread
    if len(cuts) > 0:
        entries = block_scale(rng, dims, cuts, -0.22, 0.18) * entries
    return jnp.clip(entries, min=-limit, max=limit).astype(held_as)


def setup_inputs(seed: int = 0) -> dict:
    arg_keys = jax.random.split(jax.random.key(seed), 5)
    volume = bell_draw(arg_keys[0], (SAMPLES, ND, H, W, C1), 1.0, 6.0, ((0, 4), (1, 128)))
    cotangent = bell_draw(arg_keys[1], (SAMPLES, ND2, H2, W2, CO), 1.0, 6.0, ((0, 4), (1, 128)))
    w_first = bell_draw(arg_keys[2], (3, 3, 3, C1, CM), (27 * C1) ** -0.5, 0.15625)
    w_second = bell_draw(arg_keys[3], (3, 3, 3, GIN, CO), (27 * GIN) ** -0.5, 0.3125)
    return {"volume": volume, "cotangent": cotangent, "w_first": w_first, "w_second": w_second}


def strided_section(inputs, weights):
    return lax.conv_general_dilated(inputs, weights, (2, 2, 2), ((1, 0), (1, 0), (1, 0)), dimension_numbers=('NDHWC', 'DHWIO', 'NDHWC'))

def grouped_section(inputs, weights):
    return lax.conv_general_dilated(inputs, weights, (1, 1, 1), ((1, 1), (1, 1), (1, 1)), dimension_numbers=('NDHWC', 'DHWIO', 'NDHWC'), feature_group_count=GROUPS)

def reference(volume, cotangent, w_first, w_second):
    volume_f = volume.astype(jnp.float32)
    first_f = w_first.astype(jnp.float32)
    second_f = w_second.astype(jnp.float32)
    pre = strided_section(volume_f, first_f)
    hidden = jax.nn.silu(pre).astype(jnp.bfloat16)
    result_two, pull_two = jax.vjp(grouped_section, hidden.astype(jnp.float32), second_f)
    grad_hidden_f, sum_second = pull_two(cotangent.astype(jnp.float32))
    grad_hidden = grad_hidden_f.astype(jnp.bfloat16)
    sigma = jax.nn.sigmoid(pre)
    grad_pre = (grad_hidden.astype(jnp.float32) * sigma * (1.0 + pre * (1.0 - sigma))).astype(jnp.bfloat16)
    result_one, pull_one = jax.vjp(strided_section, volume_f, first_f)
    grad_volume, sum_first = pull_one(grad_pre.astype(jnp.float32))
    scale = float(SAMPLES * ND2 * H2 * W2) ** (-0.5)
    return (grad_volume.astype(jnp.bfloat16), sum_first * scale, sum_second * scale)
```

```python
import jax
import jax.numpy as jnp
from jax import lax
from jax.experimental import pallas as pl
from jax.experimental.pallas import tpu as pltpu
from jax.sharding import PartitionSpec as P

GROUPS = 8
PAD = 32
F32 = jnp.float32
BF16 = jnp.bfloat16

NT = (((1,), (1,)), ((), ()))
NN = (((1,), (0,)), ((), ()))
TN = (((0,), (0,)), ((), ()))


def dot(a, b, dims):
    return lax.dot_general(a, b, dims, preferred_element_type=F32)


def vmem(n):
    return [pl.BlockSpec(memory_space=pltpu.VMEM)] * n


def shifted(array, by):
    size = lax.axis_size("space")
    pairs = [(i, i + by) for i in range(size) if 0 <= i + by < size]
    return lax.ppermute(array, "space", pairs)


def pair_kernel(vol, out, tmp):
    planes, rows, cols, chans = vol.shape
    step = tmp.shape[0]
    low = lax.broadcasted_iota(jnp.int32, (step, cols // 2, 2 * chans), 2) < chans

    def body(i, carry):
        p = i // (rows // step)
        r = (i % (rows // step)) * step
        tmp[:, :, 0:chans] = vol[p, pl.ds(r, step)].astype(F32)
        even = tmp[:, pl.ds(0, cols // 2, 2), :]
        odd = pltpu.roll(tmp[:, pl.ds(1, cols // 2, 2), :], chans, 2)
        out[p, pl.ds(r, step)] = jnp.where(low, even, odd).astype(BF16)
        return carry

    lax.fori_loop(0, planes * rows // step, body, 0)


def pair_columns(volume):
    planes, rows, cols, chans = volume.shape
    return pl.pallas_call(
        pair_kernel,
        out_shape=jax.ShapeDtypeStruct((planes, rows, cols // 2, 2 * chans), BF16),
        in_specs=vmem(1),
        out_specs=pl.BlockSpec(memory_space=pltpu.VMEM),
        scratch_shapes=[pltpu.VMEM((8, cols, 2 * chans), F32)],
        name="pair_columns",
        cost_estimate=pl.CostEstimate(flops=0, bytes_accessed=2 << 20, transcendentals=0),
    )(volume)


def clear(ref):
    ref[...] = jnp.zeros_like(ref)


def column_mask(shape):
    return (lax.broadcasted_iota(jnp.int32, shape, 0) & (PAD - 1)) < 24


def roll_rows(x, by):
    return pltpu.roll(x, by % x.shape[0], 0)


def group_kernel(cot_lo, cot, cot_hi, w2, gh, cpad, wd, acc):
    h2, w = cot.shape[0], cot.shape[1]
    clear(cpad)
    for p, src in enumerate((cot_lo, cot, cot_hi)):
        cpad[p, 1 : h2 + 1, 0:w] = src[...]
    lane_group = lax.broadcasted_iota(jnp.int32, (128, 256), 1) // 32
    row_group = lax.broadcasted_iota(jnp.int32, (128, 256), 0) // 16
    own = lane_group == row_group
    for tap in range(27):
        spread = jnp.concatenate([w2[tap]] * GROUPS, axis=0)
        wd[tap // 3, (tap % 3) * 128 : (tap % 3) * 128 + 128] = jnp.where(own, spread, 0.0).astype(BF16)
    for kd in range(3):
        for kr in range(3):
            x = cpad[2 - kd, 2 - kr : 2 - kr + h2].reshape(h2 * PAD, 256)
            term = dot(x, wd[kd * 3 + kr], NT)
            if kd + kr == 0:
                acc[...] = term
            else:
                acc[...] += term
    total = roll_rows(acc[:, 0:128], -1) + acc[:, 128:256] + roll_rows(acc[:, 256:384], 1)
    gh[...] = total.astype(BF16)


def group_backward(cot_lo, cot, cot_hi, w2):
    return pl.pallas_call(
        group_kernel,
        out_shape=(
            jax.ShapeDtypeStruct((16 * PAD, 128), BF16),
            jax.ShapeDtypeStruct((3, 18, PAD, 256), BF16),
        ),
        in_specs=vmem(4),
        out_specs=tuple(vmem(2)),
        scratch_shapes=[
            pltpu.VMEM((9, 384, 256), BF16),
            pltpu.VMEM((16 * PAD, 384), F32),
        ],
        name="group_backward",
        cost_estimate=pl.CostEstimate(flops=2 << 30, bytes_accessed=2 << 20, transcendentals=0),
    )(cot_lo, cot, cot_hi, w2)


def middle_kernel(lower, pairs, w1, gh, cpad, gp_out, first, second, even, odd, hid, ups):
    h2, w = 16, pairs.shape[2]
    cells = h2 * PAD
    clear(even)
    clear(odd)
    for p in range(3):
        src = lower if p == 0 else pairs.at[p - 1]
        for r in range(h2):
            even[p, r, 0:w] = src[2 * r]
            odd[p, r + 1, 0:w] = src[2 * r + 1]

    def window(kd, kr):
        if kr == 1:
            return even[kd].reshape(cells, 128)
        if kr == 0:
            return odd[kd, 0:h2].reshape(cells, 128)
        return odd[kd, 1 : h2 + 1].reshape(cells, 128)

    zeros = jnp.zeros((64, 128), BF16)
    total = None
    for kd in range(3):
        for kr in range(3):
            left = jnp.concatenate([w1[kd, kr, 1], w1[kd, kr, 2]], axis=0)
            right = jnp.concatenate([zeros, w1[kd, kr, 0]], axis=0)
            weights = jnp.concatenate([left, right], axis=1)
            term = dot(window(kd, kr), weights, NN)
            total = term if total is None else total + term
    keep = column_mask((cells, 128))
    pre = total[:, 0:128] + roll_rows(total[:, 128:256], 1)
    pre = jnp.where(keep, pre, 0.0)
    s = jax.nn.sigmoid(pre)
    hidden = (pre * s).astype(BF16).astype(F32)
    grad = gh[...].astype(F32) * s * (1.0 + pre * (1.0 - s))
    grad = jnp.where(keep, grad, 0.0).astype(BF16).astype(F32)
    ups[:, 0:128] = grad.astype(BF16)
    ups[:, 128:256] = roll_rows(grad, -1).astype(BF16)
    hid[:, 0:128] = roll_rows(hidden, 1).astype(BF16)
    hid[:, 128:256] = hidden.astype(BF16)
    hid[:, 256:384] = roll_rows(hidden, -1).astype(BF16)
    gp_out[...] = ups[:, 0:128].reshape(h2, PAD, 128)[:, 0:w]
    for kd in range(3):
        for kr in range(3):
            term = dot(window(kd, kr), ups[...], TN)
            first[kd, kr, 0] = term[64:128, 128:256]
            first[kd, kr, 1] = term[0:64, 0:128]
            first[kd, kr, 2] = term[64:128, 0:128]
    lane_group = lax.broadcasted_iota(jnp.int32, (GROUPS, 16, 256), 2) // 32
    own = lane_group == lax.broadcasted_iota(jnp.int32, (GROUPS, 16, 256), 0)
    for kd in range(3):
        for kr in range(3):
            x = cpad[2 - kd, 2 - kr : 2 - kr + h2].reshape(cells, 256)
            term = dot(hid[...], x, TN).reshape(3, GROUPS, 16, 256)
            for kc in range(3):
                second[kd, kr, kc] = jnp.sum(jnp.where(own, term[kc], 0.0), axis=0)


def middle(lower, pairs, w1, gh, cpad):
    return pl.pallas_call(
        middle_kernel,
        out_shape=(
            jax.ShapeDtypeStruct((16, 24, 128), BF16),
            jax.ShapeDtypeStruct((3, 3, 3, 64, 128), F32),
            jax.ShapeDtypeStruct((3, 3, 3, 16, 256), F32),
        ),
        in_specs=vmem(5),
        out_specs=tuple(vmem(3)),
        scratch_shapes=[
            pltpu.VMEM((3, 16, PAD, 128), BF16),
            pltpu.VMEM((3, 17, PAD, 128), BF16),
            pltpu.VMEM((16 * PAD, 384), BF16),
            pltpu.VMEM((16 * PAD, 256), BF16),
        ],
        name="middle",
        cost_estimate=pl.CostEstimate(flops=3 << 30, bytes_accessed=4 << 20, transcendentals=1 << 16),
    )(lower, pairs, w1, gh, cpad)


def input_kernel(gp, upper, w1, out, pad, tmp):
    h2, w = gp.shape[0], gp.shape[1]
    cells = h2 * PAD
    clear(pad)
    pad[0, 0:h2, 0:w] = gp[...]
    pad[1, 0:h2, 0:w] = upper[...]
    zeros = jnp.zeros((64, 128), BF16)
    low = lax.broadcasted_iota(jnp.int32, (cells, 128), 1) < 64
    for par in range(2):
        depth = ((0, 1),) if par == 0 else ((0, 2), (1, 0))
        for row_par in range(2):
            rows = ((0, 1),) if row_par == 0 else ((0, 2), (1, 0))
            total = None
            for plane, kd in depth:
                for start, kr in rows:
                    x = pad[plane, start : start + h2].reshape(cells, 128)
                    weights = jnp.concatenate(
                        [w1[kd, kr, 1], w1[kd, kr, 2], zeros, w1[kd, kr, 0]], axis=0
                    )
                    term = dot(x, weights, NT)
                    total = term if total is None else total + term
            both = total[:, 0:128] + roll_rows(total[:, 128:256], -1)
            turned = pltpu.roll(both, 64, 1)
            both = both.reshape(h2, PAD, 128)
            turned = turned.reshape(h2, PAD, 128)
            for r in range(h2):
                tmp[r % 2, pl.ds(0, w, 2), :] = both[r, 0:w]
                tmp[r % 2, pl.ds(1, w, 2), :] = turned[r, 0:w]
                out[par, 2 * r + row_par] = tmp[r % 2, :, 0:64].astype(BF16)


def input_backward(gp, upper, w1):
    return pl.pallas_call(
        input_kernel,
        out_shape=jax.ShapeDtypeStruct((2, 32, 48, 64), BF16),
        in_specs=vmem(3),
        out_specs=pl.BlockSpec(memory_space=pltpu.VMEM),
        scratch_shapes=[
            pltpu.VMEM((2, 17, PAD, 128), BF16),
            pltpu.VMEM((2, 48, 128), F32),
        ],
        name="input_backward",
        cost_estimate=pl.CostEstimate(flops=1 << 30, bytes_accessed=2 << 20, transcendentals=0),
    )(gp, upper, w1)


def on_device(volume, cotangent, w_first, w_second):
    cot = cotangent[0, 0]
    cot_lo = shifted(cot, 1)
    cot_hi = shifted(cot, -1)
    pairs = pair_columns(volume[0])
    lower = shifted(pairs[1], 1)
    gh, cpad = group_backward(cot_lo, cot, cot_hi, w_second.reshape(27, 16, 256))
    gp, first, second = middle(lower, pairs, w_first, gh, cpad)
    upper = shifted(gp, -1)
    grad_input = input_backward(gp, upper, w_first)
    sum_first, sum_second = lax.psum((first, second), ("dp", "space"))
    count = lax.axis_size("dp") * lax.axis_size("space") * 16 * 24
    scale = float(count) ** (-0.5)
    return (grad_input[None], sum_first * scale, sum_second * scale)


def solution(mesh):
    placed = (P("dp", "space", None, None, None), P("dp", "space", None, None, None), P(), P())
    return jax.shard_map(
        on_device,
        mesh=mesh,
        in_specs=placed,
        out_specs=(P("dp", "space", None, None, None), P(), P()),
        check_vma=False,
    )
```

```python
import jax
import jax.numpy as jnp
from jax import lax
from jax.experimental import pallas as pl
from jax.experimental.pallas import tpu as pltpu
from jax.sharding import Mesh
from jax.sharding import PartitionSpec as P

GROUPS = 8
SAMPLE_AXES = ("yl", "core")
DEPTH_AXES = ("z", "x", "yh")
HALF = 1296
HALF_PADDED = 1536
PAD = 32
F32 = jnp.float32
BF16 = jnp.bfloat16

NT = (((1,), (1,)), ((), ()))
NN = (((1,), (0,)), ((), ()))
TN = (((0,), (0,)), ((), ()))


def dot(a, b, dims):
    return lax.dot_general(a, b, dims, preferred_element_type=F32)


def vmem(n):
    return [pl.BlockSpec(memory_space=pltpu.VMEM)] * n


def shifted(array, by):
    size = lax.axis_size(DEPTH_AXES)
    pairs = [(i, i + by) for i in range(size) if 0 <= i + by < size]
    return lax.ppermute(array, DEPTH_AXES, pairs)


def pair_kernel(vol, out, tmp):
    planes, rows, cols, chans = vol.shape
    step = tmp.shape[0]
    low = lax.broadcasted_iota(jnp.int32, (step, cols // 2, 2 * chans), 2) < chans

    def body(i, carry):
        p = i // (rows // step)
        r = (i % (rows // step)) * step
        tmp[:, :, 0:chans] = vol[p, pl.ds(r, step)].astype(F32)
        even = tmp[:, pl.ds(0, cols // 2, 2), :]
        odd = pltpu.roll(tmp[:, pl.ds(1, cols // 2, 2), :], chans, 2)
        out[p, pl.ds(r, step)] = jnp.where(low, even, odd).astype(BF16)
        return carry

    lax.fori_loop(0, planes * rows // step, body, 0)


def pair_columns(volume):
    planes, rows, cols, chans = volume.shape
    return pl.pallas_call(
        pair_kernel,
        out_shape=jax.ShapeDtypeStruct((planes, rows, cols // 2, 2 * chans), BF16),
        in_specs=vmem(1),
        out_specs=pl.BlockSpec(memory_space=pltpu.VMEM),
        scratch_shapes=[pltpu.VMEM((8, cols, 2 * chans), F32)],
        name="pair_columns",
        cost_estimate=pl.CostEstimate(flops=0, bytes_accessed=2 << 20, transcendentals=0),
    )(volume)


def clear(ref):
    ref[...] = jnp.zeros_like(ref)


def column_mask(shape):
    return (lax.broadcasted_iota(jnp.int32, shape, 0) & (PAD - 1)) < 24


def roll_rows(x, by):
    return pltpu.roll(x, by % x.shape[0], 0)


def group_kernel(cot_lo, cot, cot_hi, w2, gh, cpad, wd, acc):
    h2, w = cot.shape[0], cot.shape[1]
    clear(cpad)
    for p, src in enumerate((cot_lo, cot, cot_hi)):
        cpad[p, 1 : h2 + 1, 0:w] = src[...]
    lane_group = lax.broadcasted_iota(jnp.int32, (128, 256), 1) // 32
    row_group = lax.broadcasted_iota(jnp.int32, (128, 256), 0) // 16
    own = lane_group == row_group
    for tap in range(27):
        spread = jnp.concatenate([w2[tap]] * GROUPS, axis=0)
        wd[tap // 3, (tap % 3) * 128 : (tap % 3) * 128 + 128] = jnp.where(own, spread, 0.0).astype(BF16)
    for kd in range(3):
        for kr in range(3):
            x = cpad[2 - kd, 2 - kr : 2 - kr + h2].reshape(h2 * PAD, 256)
            term = dot(x, wd[kd * 3 + kr], NT)
            if kd + kr == 0:
                acc[...] = term
            else:
                acc[...] += term
    total = roll_rows(acc[:, 0:128], -1) + acc[:, 128:256] + roll_rows(acc[:, 256:384], 1)
    gh[...] = total.astype(BF16)


def group_backward(cot_lo, cot, cot_hi, w2):
    return pl.pallas_call(
        group_kernel,
        out_shape=(
            jax.ShapeDtypeStruct((16 * PAD, 128), BF16),
            jax.ShapeDtypeStruct((3, 18, PAD, 256), BF16),
        ),
        in_specs=vmem(4),
        out_specs=tuple(vmem(2)),
        scratch_shapes=[
            pltpu.VMEM((9, 384, 256), BF16),
            pltpu.VMEM((16 * PAD, 384), F32),
        ],
        name="group_backward",
        cost_estimate=pl.CostEstimate(flops=2 << 30, bytes_accessed=2 << 20, transcendentals=0),
    )(cot_lo, cot, cot_hi, w2)


def row_runs(start, count):
    runs = []
    done = 0
    while done < count:
        half, row = divmod(start + done, HALF)
        size = min(count - done, HALF - row)
        runs.append((half, row, done, size))
        done += size
    return runs


def put_rows(terms, start, value):
    for half, row, done, size in row_runs(start, value.shape[0]):
        terms[half, row : row + size] = value[done : done + size]


def middle_kernel(lower, pairs, w1, gh, cpad, gp_out, terms, even, odd, hid, ups):
    h2, w = 16, pairs.shape[2]
    cells = h2 * PAD
    clear(even)
    clear(odd)
    for p in range(3):
        src = lower if p == 0 else pairs.at[p - 1]
        for r in range(h2):
            even[p, r, 0:w] = src[2 * r]
            odd[p, r + 1, 0:w] = src[2 * r + 1]

    def window(kd, kr):
        if kr == 1:
            return even[kd].reshape(cells, 128)
        if kr == 0:
            return odd[kd, 0:h2].reshape(cells, 128)
        return odd[kd, 1 : h2 + 1].reshape(cells, 128)

    zeros = jnp.zeros((64, 128), BF16)
    total = None
    for kd in range(3):
        for kr in range(3):
            left = jnp.concatenate([w1[kd, kr, 1], w1[kd, kr, 2]], axis=0)
            right = jnp.concatenate([zeros, w1[kd, kr, 0]], axis=0)
            weights = jnp.concatenate([left, right], axis=1)
            term = dot(window(kd, kr), weights, NN)
            total = term if total is None else total + term
    keep = column_mask((cells, 128))
    pre = total[:, 0:128] + roll_rows(total[:, 128:256], 1)
    pre = jnp.where(keep, pre, 0.0)
    s = jax.nn.sigmoid(pre)
    hidden = (pre * s).astype(BF16).astype(F32)
    grad = gh[...].astype(F32) * s * (1.0 + pre * (1.0 - s))
    grad = jnp.where(keep, grad, 0.0).astype(BF16).astype(F32)
    ups[:, 0:128] = grad.astype(BF16)
    ups[:, 128:256] = roll_rows(grad, -1).astype(BF16)
    hid[:, 0:128] = roll_rows(hidden, 1).astype(BF16)
    hid[:, 128:256] = hidden.astype(BF16)
    hid[:, 256:384] = roll_rows(hidden, -1).astype(BF16)
    gp_out[...] = ups[:, 0:128].reshape(h2, PAD, 128)[:, 0:w]
    for kd in range(3):
        for kr in range(3):
            term = dot(window(kd, kr), ups[...], TN)
            base = (kd * 3 + kr) * 192
            put_rows(terms, base, term[64:128, 128:256])
            put_rows(terms, base + 64, term[:, 0:128])
    lane_group = lax.broadcasted_iota(jnp.int32, (GROUPS, 16, 256), 2) // 32
    own = lane_group == lax.broadcasted_iota(jnp.int32, (GROUPS, 16, 256), 0)
    for kd in range(3):
        for kr in range(3):
            x = cpad[2 - kd, 2 - kr : 2 - kr + h2].reshape(cells, 256)
            term = dot(hid[...], x, TN).reshape(3, GROUPS, 16, 256)
            for kc in range(3):
                part = jnp.sum(jnp.where(own, term[kc], 0.0), axis=0)
                base = 1728 + ((kd * 3 + kr) * 3 + kc) * 16
                put_rows(terms, base, part[:, 0:128])
                put_rows(terms, base + 432, part[:, 128:256])


def middle(lower, pairs, w1, gh, cpad):
    return pl.pallas_call(
        middle_kernel,
        out_shape=(
            jax.ShapeDtypeStruct((16, 24, 128), BF16),
            jax.ShapeDtypeStruct((2, HALF_PADDED, 128), F32),
        ),
        in_specs=vmem(5),
        out_specs=tuple(vmem(2)),
        scratch_shapes=[
            pltpu.VMEM((3, 16, PAD, 128), BF16),
            pltpu.VMEM((3, 17, PAD, 128), BF16),
            pltpu.VMEM((16 * PAD, 384), BF16),
            pltpu.VMEM((16 * PAD, 256), BF16),
        ],
        name="middle",
        cost_estimate=pl.CostEstimate(flops=3 << 30, bytes_accessed=4 << 20, transcendentals=1 << 16),
    )(lower, pairs, w1, gh, cpad)


def input_kernel(gp, upper, w1, out, pad, tmp):
    h2, w = gp.shape[0], gp.shape[1]
    cells = h2 * PAD
    clear(pad)
    pad[0, 0:h2, 0:w] = gp[...]
    pad[1, 0:h2, 0:w] = upper[...]
    zeros = jnp.zeros((64, 128), BF16)
    for par in range(2):
        depth = ((0, 1),) if par == 0 else ((0, 2), (1, 0))
        for row_par in range(2):
            rows = ((0, 1),) if row_par == 0 else ((0, 2), (1, 0))
            total = None
            for plane, kd in depth:
                for start, kr in rows:
                    x = pad[plane, start : start + h2].reshape(cells, 128)
                    weights = jnp.concatenate(
                        [w1[kd, kr, 1], w1[kd, kr, 2], zeros, w1[kd, kr, 0]], axis=0
                    )
                    term = dot(x, weights, NT)
                    total = term if total is None else total + term
            both = total[:, 0:128] + roll_rows(total[:, 128:256], -1)
            turned = pltpu.roll(both, 64, 1)
            both = both.reshape(h2, PAD, 128)
            turned = turned.reshape(h2, PAD, 128)
            for r in range(h2):
                tmp[r % 2, pl.ds(0, w, 2), :] = both[r, 0:w]
                tmp[r % 2, pl.ds(1, w, 2), :] = turned[r, 0:w]
                out[par, 2 * r + row_par] = tmp[r % 2, :, 0:64].astype(BF16)


def input_backward(gp, upper, w1):
    return pl.pallas_call(
        input_kernel,
        out_shape=jax.ShapeDtypeStruct((2, 32, 48, 64), BF16),
        in_specs=vmem(3),
        out_specs=pl.BlockSpec(memory_space=pltpu.VMEM),
        scratch_shapes=[
            pltpu.VMEM((2, 17, PAD, 128), BF16),
            pltpu.VMEM((2, 48, 128), F32),
        ],
        name="input_backward",
        cost_estimate=pl.CostEstimate(flops=1 << 30, bytes_accessed=2 << 20, transcendentals=0),
    )(gp, upper, w1)


def unpack_kernel(summed, first, second):
    for tap in range(27):
        for half, row, done, size in row_runs(tap * 64, 64):
            first[tap, done : done + size] = summed[half, row : row + size]
        for side in range(2):
            for half, row, done, size in row_runs(1728 + side * 432 + tap * 16, 16):
                second[tap, done : done + size, side * 128 : side * 128 + 128] = summed[
                    half, row : row + size
                ]


def unpack(summed):
    return pl.pallas_call(
        unpack_kernel,
        out_shape=(
            jax.ShapeDtypeStruct((27, 64, 128), F32),
            jax.ShapeDtypeStruct((27, 16, 256), F32),
        ),
        in_specs=vmem(1),
        out_specs=tuple(vmem(2)),
        name="unpack",
        cost_estimate=pl.CostEstimate(flops=0, bytes_accessed=3 << 20, transcendentals=0),
    )(summed)


def exchange(blocks, axes):
    return lax.all_to_all(blocks, axes, split_axis=0, concat_axis=0, tiled=True)


def spread(block, axes):
    count = lax.axis_size(axes)
    return exchange(jnp.broadcast_to(block[None], (count,) + block.shape), axes)


def sum_everywhere(terms, scale):
    plane = ("z", "x")
    line = ("yl", "yh")
    half = jnp.sum(exchange(terms, "core"), axis=0)
    count = lax.axis_size(plane)
    mine = jnp.sum(exchange(half.reshape(count, HALF_PADDED // count, 128), plane), axis=0)
    mine = jnp.sum(spread(mine, line), axis=0) * scale
    half = spread(mine, plane).reshape(HALF_PADDED, 128)
    return spread(half, "core")


def on_device(volume, cotangent, w_first, w_second):
    cot = cotangent[0, 0]
    cot_lo = shifted(cot, 1)
    cot_hi = shifted(cot, -1)
    pairs = pair_columns(volume[0])
    lower = shifted(pairs[1], 1)
    gh, cpad = group_backward(cot_lo, cot, cot_hi, w_second.reshape(27, 16, 256))
    gp, terms = middle(lower, pairs, w_first, gh, cpad)
    upper = shifted(gp, -1)
    grad_input = input_backward(gp, upper, w_first)
    count = lax.axis_size(SAMPLE_AXES) * lax.axis_size(DEPTH_AXES) * 16 * 24
    scale = float(count) ** (-0.5)
    first, second = unpack(sum_everywhere(terms, scale))
    return (grad_input[None], first.reshape(3, 3, 3, 64, 128), second.reshape(3, 3, 3, 16, 256))


def solution(mesh):
    fine = Mesh(mesh.devices.reshape(2, 2, 8, 4, 4), SAMPLE_AXES + DEPTH_AXES)
    split = P(SAMPLE_AXES, DEPTH_AXES, None, None, None)
    return jax.shard_map(
        on_device,
        mesh=fine,
        in_specs=(split, split, P(), P()),
        out_specs=(split, P(), P()),
        check_vma=False,
    )
```

```python
import jax
import jax.numpy as jnp
from jax import lax
from jax.experimental import pallas as pl
from jax.experimental.pallas import tpu as pltpu
from jax.sharding import Mesh
from jax.sharding import PartitionSpec as P

GROUPS = 8
SAMPLE_AXES = ("yl", "core")
DEPTH_AXES = ("z", "x", "yh")
HALF = 1296
HALF_PADDED = 1536
PAD = 32
F32 = jnp.float32
BF16 = jnp.bfloat16

NT = (((1,), (1,)), ((), ()))
NN = (((1,), (0,)), ((), ()))
TN = (((0,), (0,)), ((), ()))


def dot(a, b, dims):
    return lax.dot_general(a, b, dims, preferred_element_type=F32)


def vmem(n):
    return [pl.BlockSpec(memory_space=pltpu.VMEM)] * n


def shifted(array, by):
    size = lax.axis_size(DEPTH_AXES)
    pairs = [(i, i + by) for i in range(size) if 0 <= i + by < size]
    return lax.ppermute(array, DEPTH_AXES, pairs)


def pair_kernel(vol, out, tmp):
    planes, rows, cols, chans = vol.shape
    step = tmp.shape[0]
    low = lax.broadcasted_iota(jnp.int32, (step, cols // 2, 2 * chans), 2) < chans

    def body(i, carry):
        p = i // (rows // step)
        r = (i % (rows // step)) * step
        tmp[:, :, 0:chans] = vol[p, pl.ds(r, step)].astype(F32)
        even = tmp[:, pl.ds(0, cols // 2, 2), :]
        odd = pltpu.roll(tmp[:, pl.ds(1, cols // 2, 2), :], chans, 2)
        out[p, pl.ds(r, step)] = jnp.where(low, even, odd).astype(BF16)
        return carry

    lax.fori_loop(0, planes * rows // step, body, 0)


def pair_columns(volume):
    planes, rows, cols, chans = volume.shape
    return pl.pallas_call(
        pair_kernel,
        out_shape=jax.ShapeDtypeStruct((planes, rows, cols // 2, 2 * chans), BF16),
        in_specs=vmem(1),
        out_specs=pl.BlockSpec(memory_space=pltpu.VMEM),
        scratch_shapes=[pltpu.VMEM((8, cols, 2 * chans), F32)],
        name="pair_columns",
        cost_estimate=pl.CostEstimate(flops=0, bytes_accessed=2 << 20, transcendentals=0),
    )(volume)


def clear(ref):
    ref[...] = jnp.zeros_like(ref)


def column_mask(shape):
    return (lax.broadcasted_iota(jnp.int32, shape, 0) & (PAD - 1)) < 24


def roll_rows(x, by):
    return pltpu.roll(x, by % x.shape[0], 0)


def group_kernel(cot_lo, cot, cot_hi, w2, gh, cpad, wd, acc):
    h2, w = cot.shape[0], cot.shape[1]
    clear(cpad)
    for p, src in enumerate((cot_lo, cot, cot_hi)):
        cpad[p, 1 : h2 + 1, 0:w] = src[...]
    lane_group = lax.broadcasted_iota(jnp.int32, (128, 256), 1) // 32
    row_group = lax.broadcasted_iota(jnp.int32, (128, 256), 0) // 16
    own = lane_group == row_group
    for tap in range(27):
        spread = jnp.concatenate([w2[tap]] * GROUPS, axis=0)
        wd[tap // 3, (tap % 3) * 128 : (tap % 3) * 128 + 128] = jnp.where(own, spread, 0.0).astype(BF16)
    for kd in range(3):
        for kr in range(3):
            x = cpad[2 - kd, 2 - kr : 2 - kr + h2].reshape(h2 * PAD, 256)
            term = dot(x, wd[kd * 3 + kr], NT)
            if kd + kr == 0:
                acc[...] = term
            else:
                acc[...] += term
    total = roll_rows(acc[:, 0:128], -1) + acc[:, 128:256] + roll_rows(acc[:, 256:384], 1)
    gh[...] = total.astype(BF16)


def group_backward(cot_lo, cot, cot_hi, w2):
    return pl.pallas_call(
        group_kernel,
        out_shape=(
            jax.ShapeDtypeStruct((16 * PAD, 128), BF16),
            jax.ShapeDtypeStruct((3, 18, PAD, 256), BF16),
        ),
        in_specs=vmem(4),
        out_specs=tuple(vmem(2)),
        scratch_shapes=[
            pltpu.VMEM((9, 384, 256), BF16),
            pltpu.VMEM((16 * PAD, 384), F32),
        ],
        name="group_backward",
        cost_estimate=pl.CostEstimate(flops=2 << 30, bytes_accessed=2 << 20, transcendentals=0),
    )(cot_lo, cot, cot_hi, w2)


def row_runs(start, count):
    runs = []
    done = 0
    while done < count:
        half, row = divmod(start + done, HALF)
        size = min(count - done, HALF - row)
        runs.append((half, row, done, size))
        done += size
    return runs


def put_rows(terms, start, value):
    for half, row, done, size in row_runs(start, value.shape[0]):
        terms[half, row : row + size] = value[done : done + size].astype(BF16)


def middle_kernel(lower, pairs, w1, gh, cpad, gp_out, terms, even, odd, hid, ups):
    h2, w = 16, pairs.shape[2]
    cells = h2 * PAD
    clear(even)
    clear(odd)
    for p in range(3):
        src = lower if p == 0 else pairs.at[p - 1]
        for r in range(h2):
            even[p, r, 0:w] = src[2 * r]
            odd[p, r + 1, 0:w] = src[2 * r + 1]

    def window(kd, kr):
        if kr == 1:
            return even[kd].reshape(cells, 128)
        if kr == 0:
            return odd[kd, 0:h2].reshape(cells, 128)
        return odd[kd, 1 : h2 + 1].reshape(cells, 128)

    zeros = jnp.zeros((64, 128), BF16)
    total = None
    for kd in range(3):
        for kr in range(3):
            left = jnp.concatenate([w1[kd, kr, 1], w1[kd, kr, 2]], axis=0)
            right = jnp.concatenate([zeros, w1[kd, kr, 0]], axis=0)
            weights = jnp.concatenate([left, right], axis=1)
            term = dot(window(kd, kr), weights, NN)
            total = term if total is None else total + term
    keep = column_mask((cells, 128))
    pre = total[:, 0:128] + roll_rows(total[:, 128:256], 1)
    pre = jnp.where(keep, pre, 0.0)
    s = jax.nn.sigmoid(pre)
    hidden = (pre * s).astype(BF16).astype(F32)
    grad = gh[...].astype(F32) * s * (1.0 + pre * (1.0 - s))
    grad = jnp.where(keep, grad, 0.0).astype(BF16).astype(F32)
    ups[:, 0:128] = grad.astype(BF16)
    ups[:, 128:256] = roll_rows(grad, -1).astype(BF16)
    hid[:, 0:128] = roll_rows(hidden, 1).astype(BF16)
    hid[:, 128:256] = hidden.astype(BF16)
    hid[:, 256:384] = roll_rows(hidden, -1).astype(BF16)
    gp_out[...] = ups[:, 0:128].reshape(h2, PAD, 128)[:, 0:w]
    for kd in range(3):
        for kr in range(3):
            term = dot(window(kd, kr), ups[...], TN)
            base = (kd * 3 + kr) * 192
            put_rows(terms, base, term[64:128, 128:256])
            put_rows(terms, base + 64, term[:, 0:128])
    lane_group = lax.broadcasted_iota(jnp.int32, (GROUPS, 16, 256), 2) // 32
    own = lane_group == lax.broadcasted_iota(jnp.int32, (GROUPS, 16, 256), 0)
    for kd in range(3):
        for kr in range(3):
            x = cpad[2 - kd, 2 - kr : 2 - kr + h2].reshape(cells, 256)
            term = dot(hid[...], x, TN).reshape(3, GROUPS, 16, 256)
            for kc in range(3):
                part = jnp.sum(jnp.where(own, term[kc], 0.0), axis=0)
                base = 1728 + ((kd * 3 + kr) * 3 + kc) * 16
                put_rows(terms, base, part[:, 0:128])
                put_rows(terms, base + 432, part[:, 128:256])


def middle(lower, pairs, w1, gh, cpad):
    return pl.pallas_call(
        middle_kernel,
        out_shape=(
            jax.ShapeDtypeStruct((16, 24, 128), BF16),
            jax.ShapeDtypeStruct((2, HALF_PADDED, 128), BF16),
        ),
        in_specs=vmem(5),
        out_specs=tuple(vmem(2)),
        scratch_shapes=[
            pltpu.VMEM((3, 16, PAD, 128), BF16),
            pltpu.VMEM((3, 17, PAD, 128), BF16),
            pltpu.VMEM((16 * PAD, 384), BF16),
            pltpu.VMEM((16 * PAD, 256), BF16),
        ],
        name="middle",
        cost_estimate=pl.CostEstimate(flops=3 << 30, bytes_accessed=4 << 20, transcendentals=1 << 16),
    )(lower, pairs, w1, gh, cpad)


def input_kernel(gp, upper, w1, out, pad, tmp):
    h2, w = gp.shape[0], gp.shape[1]
    cells = h2 * PAD
    clear(pad)
    pad[0, 0:h2, 0:w] = gp[...]
    pad[1, 0:h2, 0:w] = upper[...]
    zeros = jnp.zeros((64, 128), BF16)
    for par in range(2):
        depth = ((0, 1),) if par == 0 else ((0, 2), (1, 0))
        for row_par in range(2):
            rows = ((0, 1),) if row_par == 0 else ((0, 2), (1, 0))
            total = None
            for plane, kd in depth:
                for start, kr in rows:
                    x = pad[plane, start : start + h2].reshape(cells, 128)
                    weights = jnp.concatenate(
                        [w1[kd, kr, 1], w1[kd, kr, 2], zeros, w1[kd, kr, 0]], axis=0
                    )
                    term = dot(x, weights, NT)
                    total = term if total is None else total + term
            both = total[:, 0:128] + roll_rows(total[:, 128:256], -1)
            turned = pltpu.roll(both, 64, 1)
            both = both.reshape(h2, PAD, 128)
            turned = turned.reshape(h2, PAD, 128)
            for r in range(h2):
                tmp[r % 2, pl.ds(0, w, 2), :] = both[r, 0:w]
                tmp[r % 2, pl.ds(1, w, 2), :] = turned[r, 0:w]
                out[par, 2 * r + row_par] = tmp[r % 2, :, 0:64].astype(BF16)


def input_backward(gp, upper, w1):
    return pl.pallas_call(
        input_kernel,
        out_shape=jax.ShapeDtypeStruct((2, 32, 48, 64), BF16),
        in_specs=vmem(3),
        out_specs=pl.BlockSpec(memory_space=pltpu.VMEM),
        scratch_shapes=[
            pltpu.VMEM((2, 17, PAD, 128), BF16),
            pltpu.VMEM((2, 48, 128), F32),
        ],
        name="input_backward",
        cost_estimate=pl.CostEstimate(flops=1 << 30, bytes_accessed=2 << 20, transcendentals=0),
    )(gp, upper, w1)


def unpack_kernel(summed, first, second):
    for tap in range(27):
        for half, row, done, size in row_runs(tap * 64, 64):
            first[tap, done : done + size] = summed[half, row : row + size].astype(F32)
        for side in range(2):
            for half, row, done, size in row_runs(1728 + side * 432 + tap * 16, 16):
                second[tap, done : done + size, side * 128 : side * 128 + 128] = summed[
                    half, row : row + size
                ].astype(F32)


def unpack(summed):
    return pl.pallas_call(
        unpack_kernel,
        out_shape=(
            jax.ShapeDtypeStruct((27, 64, 128), F32),
            jax.ShapeDtypeStruct((27, 16, 256), F32),
        ),
        in_specs=vmem(1),
        out_specs=tuple(vmem(2)),
        name="unpack",
        cost_estimate=pl.CostEstimate(flops=0, bytes_accessed=3 << 20, transcendentals=0),
    )(summed)


def exchange(blocks, axes):
    return lax.all_to_all(blocks, axes, split_axis=0, concat_axis=0, tiled=True)


def spread(block, axes):
    count = lax.axis_size(axes)
    return exchange(jnp.broadcast_to(block[None], (count,) + block.shape), axes)


def added(blocks):
    return jnp.sum(blocks.astype(F32), axis=0)


def sum_everywhere(terms, scale):
    plane = ("z", "x")
    line = ("yl", "yh")
    count = lax.axis_size(plane)
    half = added(exchange(terms, "core")).astype(BF16)
    mine = added(exchange(half.reshape(count, HALF_PADDED // count, 128), plane))
    mine = (added(spread(mine, line)) * scale).astype(BF16)
    half = spread(mine, plane).reshape(HALF_PADDED, 128)
    return spread(half, "core")


def on_device(volume, cotangent, w_first, w_second):
    cot = cotangent[0, 0]
    cot_lo = shifted(cot, 1)
    cot_hi = shifted(cot, -1)
    pairs = pair_columns(volume[0])
    lower = shifted(pairs[1], 1)
    gh, cpad = group_backward(cot_lo, cot, cot_hi, w_second.reshape(27, 16, 256))
    gp, terms = middle(lower, pairs, w_first, gh, cpad)
    upper = shifted(gp, -1)
    grad_input = input_backward(gp, upper, w_first)
    count = lax.axis_size(SAMPLE_AXES) * lax.axis_size(DEPTH_AXES) * 16 * 24
    scale = float(count) ** (-0.5)
    first, second = unpack(sum_everywhere(terms, scale))
    return (grad_input[None], first.reshape(3, 3, 3, 64, 128), second.reshape(3, 3, 3, 16, 256))


def solution(mesh):
    fine = Mesh(mesh.devices.reshape(2, 2, 8, 4, 4), SAMPLE_AXES + DEPTH_AXES)
    split = P(SAMPLE_AXES, DEPTH_AXES, None, None, None)
    return jax.shard_map(
        on_device,
        mesh=fine,
        in_specs=(split, split, P(), P()),
        out_specs=(split, P(), P()),
        check_vma=False,
    )
```

```python
import functools

import jax
import jax.numpy as jnp
from jax import lax
from jax.experimental import pallas as pl
from jax.experimental.pallas import tpu as pltpu
from jax.sharding import Mesh
from jax.sharding import PartitionSpec as P

GROUPS = 8
SAMPLE_AXES = ("yl", "core")
DEPTH_AXES = ("z", "x", "yh")
TAPS = 27
CHUNK = 48
PAD = 32
F32 = jnp.float32
BF16 = jnp.bfloat16

NT = (((1,), (1,)), ((), ()))
NN = (((1,), (0,)), ((), ()))
TN = (((0,), (0,)), ((), ()))


def dot(a, b, dims):
    return lax.dot_general(a, b, dims, preferred_element_type=F32)


def vmem(n):
    return [pl.BlockSpec(memory_space=pltpu.VMEM)] * n


def shifted(array, by):
    size = lax.axis_size(DEPTH_AXES)
    pairs = [(i, i + by) for i in range(size) if 0 <= i + by < size]
    return lax.ppermute(array, DEPTH_AXES, pairs)


def clear(ref):
    ref[...] = jnp.zeros_like(ref)


def roll_rows(x, by):
    return pltpu.roll(x, by % x.shape[0], 0)


def half_turn(x):
    return pltpu.roll(x, 64, x.ndim - 1)


def low_lanes(shape):
    return lax.broadcasted_iota(jnp.int32, shape, len(shape) - 1) < 64


def pair_rows(plane, out, tmp):
    step = tmp.shape[0]
    low = low_lanes((step, 24, 128))

    def body(i, carry):
        r = i * step
        tmp[:, :, 0:64] = plane[pl.ds(r, step)].astype(F32)
        even = tmp[:, pl.ds(0, 24, 2), :]
        odd = half_turn(tmp[:, pl.ds(1, 24, 2), :])
        out[pl.ds(r, step)] = jnp.where(low, even, odd).astype(BF16)
        return carry

    lax.fori_loop(0, plane.shape[0] // step, body, 0)


def pack_kernel(vol, cot, out, tmp):
    pair_rows(vol.at[0, 0], out.at[0:32], tmp)
    out[32:48] = cot[:, :, 0:128]
    out[48:64] = cot[:, :, 128:256]


def pack(volume, cot):
    return pl.pallas_call(
        pack_kernel,
        grid=(1,),
        out_shape=jax.ShapeDtypeStruct((64, 24, 128), BF16),
        in_specs=[
            pl.BlockSpec((1, 1, 32, 48, 64), lambda i: (0, 1, 0, 0, 0)),
            pl.BlockSpec((16, 24, 256), lambda i: (0, 0, 0)),
        ],
        out_specs=pl.BlockSpec((64, 24, 128), lambda i: (0, 0, 0)),
        scratch_shapes=[pltpu.VMEM((8, 48, 128), F32)],
        name="pack",
        cost_estimate=pl.CostEstimate(flops=0, bytes_accessed=2 << 20, transcendentals=0),
    )(volume, cot)


def split_rows(pairs, even, odd):
    for r in range(16):
        even[r, 0:24] = pairs[2 * r]
        odd[r + 1, 0:24] = pairs[2 * r + 1]


def window(even, odd, kr):
    rows = even[...] if kr == 1 else odd[kr // 2 : kr // 2 + 16]
    return rows.reshape(16 * PAD, 128)


def strided_terms(windows, w1):
    zeros = jnp.zeros((64, 128), BF16)

    def weights(kd, kr):
        left = jnp.concatenate([w1[kd, kr, 1], w1[kd, kr, 2]], axis=0)
        right = jnp.concatenate([zeros, w1[kd, kr, 0]], axis=0)
        return jnp.concatenate([left, right], axis=1)

    total = None
    for i in range(0, len(windows), 2):
        pair = windows[i : i + 2]
        x = jnp.concatenate([p[2] for p in pair], axis=1) if len(pair) == 2 else pair[0][2]
        w = jnp.concatenate([weights(p[0], p[1]) for p in pair], axis=0)
        term = dot(x, w, NN)
        total = term if total is None else total + term
    return total[:, 0:128] + roll_rows(total[:, 128:256], 1)


def own_group():
    lane_group = lax.broadcasted_iota(jnp.int32, (128, 256), 1) // 32
    return lane_group == lax.broadcasted_iota(jnp.int32, (128, 256), 0) // 16


def put_weights(w2, kd, wd):
    own = own_group()
    for kr in range(3):
        for kc in range(3):
            spread = jnp.concatenate([w2[kd * 9 + kr * 3 + kc]] * GROUPS, axis=0)
            wd[kr, kc * 128 : kc * 128 + 128] = jnp.where(own, spread, 0.0).astype(BF16)


def cot_window(cpad, kr):
    return cpad[2 - kr : 18 - kr].reshape(16 * PAD, 256)


def grouped_terms(cpad, wd):
    total = None
    for kr in range(3):
        term = dot(cot_window(cpad, kr), wd[kr], NT)
        total = term if total is None else total + term
    return total


def join_columns(total):
    return roll_rows(total[:, 0:128], -1) + total[:, 128:256] + roll_rows(total[:, 256:384], 1)


def early_kernel(vol, packed, cot, w1, w2, pre, gh, even, odd, tmp, pairs, cpad, wd):
    clear(even)
    clear(odd)
    clear(cpad)
    pair_rows(vol.at[0, 0], pairs, tmp)
    split_rows(pairs, even.at[0], odd.at[0])
    split_rows(packed, even.at[1], odd.at[1])
    cpad[1:17, 0:24] = cot[...]
    windows = []
    for kd in (1, 2):
        for kr in range(3):
            windows.append((kd, kr, window(even.at[kd - 1], odd.at[kd - 1], kr)))
    pre[...] = strided_terms(windows, w1)
    put_weights(w2, 1, wd)
    gh[...] = join_columns(grouped_terms(cpad, wd))


def early(volume, packed, cot, w1, w2):
    whole = lambda *shape: pl.BlockSpec(shape, lambda i: (0,) * len(shape))
    return pl.pallas_call(
        early_kernel,
        grid=(1,),
        out_shape=(
            jax.ShapeDtypeStruct((16 * PAD, 128), F32),
            jax.ShapeDtypeStruct((16 * PAD, 128), F32),
            jax.ShapeDtypeStruct((2, 16, PAD, 128), BF16),
            jax.ShapeDtypeStruct((2, 17, PAD, 128), BF16),
        ),
        in_specs=[
            whole(1, 1, 32, 48, 64),
            whole(64, 24, 128),
            whole(16, 24, 256),
            whole(3, 3, 3, 64, 128),
            whole(27, 16, 256),
        ],
        out_specs=(
            whole(16 * PAD, 128),
            whole(16 * PAD, 128),
            whole(2, 16, PAD, 128),
            whole(2, 17, PAD, 128),
        ),
        scratch_shapes=[
            pltpu.VMEM((8, 48, 128), F32),
            pltpu.VMEM((32, 24, 128), BF16),
            pltpu.VMEM((18, PAD, 256), BF16),
            pltpu.VMEM((3, 384, 256), BF16),
        ],
        name="early",
        cost_estimate=pl.CostEstimate(flops=1 << 30, bytes_accessed=2 << 20, transcendentals=0),
    )(volume, packed, cot, w1, w2)


def middle_kernel(
    core, got, cot, cot_hi, pre_part, gh_part, even12, odd12, w1, w2,
    gp_out, keep_out, send_out,
    even0, odd0, cpad, wd, hid, ups, hid_t, ups_t,
):
    cells = 16 * PAD
    clear(even0)
    clear(odd0)
    clear(cpad)
    split_rows(got, even0, odd0)
    cpad[0, 1:17, 0:24, 0:128] = got[32:48]
    cpad[0, 1:17, 0:24, 128:256] = got[48:64]
    cpad[1, 1:17, 0:24] = cot[...]
    cpad[2, 1:17, 0:24] = cot_hi[...]
    put_weights(w2, 0, wd.at[0])
    put_weights(w2, 2, wd.at[1])
    total = grouped_terms(cpad.at[2], wd.at[0]) + grouped_terms(cpad.at[0], wd.at[1])
    gh = (join_columns(total) + gh_part[...]).astype(BF16).astype(F32)
    windows = [[window(even0, odd0, kr) for kr in range(3)]]
    for p in range(2):
        windows.append([window(even12.at[p], odd12.at[p], kr) for kr in range(3)])
    pre = strided_terms([(0, kr, windows[0][kr]) for kr in range(3)], w1) + pre_part[...]
    inside = (lax.broadcasted_iota(jnp.int32, (cells, 128), 0) & (PAD - 1)) < 24
    pre = jnp.where(inside, pre, 0.0)
    s = jax.nn.sigmoid(pre)
    hidden = (pre * s).astype(BF16).astype(F32)
    grad = gh * s * (1.0 + pre * (1.0 - s))
    grad = jnp.where(inside, grad, 0.0).astype(BF16).astype(F32)
    ups[:, 0:128] = grad.astype(BF16)
    ups[:, 128:256] = roll_rows(grad, -1).astype(BF16)
    hid[:, 0:128] = roll_rows(hidden, 1).astype(BF16)
    hid[:, 128:256] = hidden.astype(BF16)
    hid[:, 256:384] = roll_rows(hidden, -1).astype(BF16)
    gp_out[...] = ups[:, 0:128].reshape(16, PAD, 128)[:, 0:24]
    ups_t[...] = ups[...].T
    hid_t[...] = hid[...].T
    first_core = core[0] == 0

    def put(tap, row, half0, half1):
        size = half0.shape[0]
        keep_out[tap, row : row + size] = jnp.where(first_core, half0, half1)
        send_out[tap, row : row + size] = jnp.where(first_core, half1, half0).astype(BF16)

    low = low_lanes((32, 128))
    flat = [windows[kd][kr] for kd in range(3) for kr in range(3)]
    for i in range(0, 9, 2):
        pair = flat[i : i + 2]
        x = jnp.concatenate(pair, axis=1) if len(pair) == 2 else pair[0]
        term = dot(ups_t[...], x, NN)
        for j in range(len(pair)):
            part = term[:, j * 128 : j * 128 + 128]
            tap = (i + j) * 3
            centre, side = [], []
            right = []
            for half in range(2):
                p = part[half * 64 : half * 64 + 32]
                q = part[half * 64 + 32 : half * 64 + 64]
                p1 = part[128 + half * 64 : 128 + half * 64 + 32]
                q1 = part[128 + half * 64 + 32 : 128 + half * 64 + 64]
                centre.append(jnp.where(low, p, half_turn(q)))
                right.append(jnp.where(low, half_turn(p), q))
                side.append(jnp.where(low, half_turn(p1), q1))
            put(tap, 0, *side)
            put(tap + 1, 0, *centre)
            put(tap + 2, 0, *right)
    own = own_group()
    for kd in range(3):
        for kr in range(3):
            term = dot(hid_t[...], cot_window(cpad.at[2 - kd], kr), NN)
            for kc in range(3):
                part = jnp.where(own, term[kc * 128 : kc * 128 + 128], 0.0)
                part = jnp.sum(part.reshape(GROUPS, 16, 256), axis=0)
                put((kd * 3 + kr) * 3 + kc, 32, part[:, 0:128], part[:, 128:256])
    keep_out[TAPS:32] = jnp.zeros((32 - TAPS, CHUNK, 128), F32)
    send_out[TAPS:32] = jnp.zeros((32 - TAPS, CHUNK, 128), BF16)


def middle(core, got, cot, cot_hi, pre, gh, even, odd, w1, w2):
    return pl.pallas_call(
        middle_kernel,
        out_shape=(
            jax.ShapeDtypeStruct((16, 24, 128), BF16),
            jax.ShapeDtypeStruct((32, CHUNK, 128), F32),
            jax.ShapeDtypeStruct((32, CHUNK, 128), BF16),
        ),
        in_specs=[pl.BlockSpec(memory_space=pltpu.SMEM)] + vmem(9),
        out_specs=tuple(vmem(3)),
        scratch_shapes=[
            pltpu.VMEM((16, PAD, 128), BF16),
            pltpu.VMEM((17, PAD, 128), BF16),
            pltpu.VMEM((3, 18, PAD, 256), BF16),
            pltpu.VMEM((2, 3, 384, 256), BF16),
            pltpu.VMEM((16 * PAD, 384), BF16),
            pltpu.VMEM((16 * PAD, 256), BF16),
            pltpu.VMEM((384, 16 * PAD), BF16),
            pltpu.VMEM((256, 16 * PAD), BF16),
        ],
        name="middle",
        cost_estimate=pl.CostEstimate(flops=3 << 30, bytes_accessed=4 << 20, transcendentals=1 << 16),
    )(core, got, cot, cot_hi, pre, gh, even, odd, w1, w2)


def input_kernel(gp, upper, w1, out, pad, tmp):
    h2, w = gp.shape[0], gp.shape[1]
    cells = h2 * PAD
    clear(pad)
    pad[0, 0:h2, 0:w] = gp[...]
    pad[1, 0:h2, 0:w] = upper[...]
    zeros = jnp.zeros((64, 128), BF16)
    for par in range(2):
        depth = ((0, 1),) if par == 0 else ((0, 2), (1, 0))
        for row_par in range(2):
            rows = ((0, 1),) if row_par == 0 else ((0, 2), (1, 0))
            total = None
            for plane, kd in depth:
                for start, kr in rows:
                    x = pad[plane, start : start + h2].reshape(cells, 128)
                    weights = jnp.concatenate(
                        [w1[kd, kr, 1], w1[kd, kr, 2], zeros, w1[kd, kr, 0]], axis=0
                    )
                    term = dot(x, weights, NT)
                    total = term if total is None else total + term
            both = total[:, 0:128] + roll_rows(total[:, 128:256], -1)
            turned = pltpu.roll(both, 64, 1)
            both = both.reshape(h2, PAD, 128)
            turned = turned.reshape(h2, PAD, 128)
            for r in range(h2):
                tmp[r % 2, pl.ds(0, w, 2), :] = both[r, 0:w]
                tmp[r % 2, pl.ds(1, w, 2), :] = turned[r, 0:w]
                out[par, 2 * r + row_par] = tmp[r % 2, :, 0:64].astype(BF16)


def input_backward(gp, upper, w1):
    return pl.pallas_call(
        input_kernel,
        out_shape=jax.ShapeDtypeStruct((2, 32, 48, 64), BF16),
        in_specs=vmem(3),
        out_specs=pl.BlockSpec(memory_space=pltpu.VMEM),
        scratch_shapes=[
            pltpu.VMEM((2, 17, PAD, 128), BF16),
            pltpu.VMEM((2, 48, 128), F32),
        ],
        name="input_backward",
        cost_estimate=pl.CostEstimate(flops=1 << 30, bytes_accessed=2 << 20, transcendentals=0),
    )(gp, upper, w1)


def finish_kernel(scale, blocks, out):
    total = jnp.sum(blocks[...], axis=0) * scale
    packed = total[0:32]
    flipped = packed.T
    turned = jnp.concatenate([flipped[0:64], flipped[64:128]], axis=1)
    top = jnp.concatenate([turned[0:32], turned[32:64]], axis=1)
    mine = jnp.concatenate([top, total[32:48]], axis=0).astype(BF16)
    out[...] = jnp.broadcast_to(mine[None], out.shape)


def finish(blocks, count, scale):
    return pl.pallas_call(
        functools.partial(finish_kernel, scale),
        out_shape=jax.ShapeDtypeStruct((count, CHUNK, 128), BF16),
        in_specs=vmem(1),
        out_specs=pl.BlockSpec(memory_space=pltpu.VMEM),
        name="finish",
        cost_estimate=pl.CostEstimate(flops=1 << 16, bytes_accessed=1 << 20, transcendentals=0),
    )(blocks)


def unpack_kernel(core, mine, other, first, second):
    first_core = core[0] == 0
    low = low_lanes((32, 128))
    for tap in range(TAPS):
        a = mine[tap].astype(F32)
        b = other[tap].astype(F32)
        half0 = jnp.where(first_core, a, b)
        half1 = jnp.where(first_core, b, a)
        top, bottom = half0[0:32], half1[0:32]
        first[tap, 0:32] = jnp.where(low, top, half_turn(bottom))
        first[tap, 32:64] = jnp.where(low, half_turn(top), bottom)
        second[tap, :, 0:128] = half0[32:48]
        second[tap, :, 128:256] = half1[32:48]


def unpack(core, mine, other):
    return pl.pallas_call(
        unpack_kernel,
        out_shape=(
            jax.ShapeDtypeStruct((TAPS, 64, 128), F32),
            jax.ShapeDtypeStruct((TAPS, 16, 256), F32),
        ),
        in_specs=[pl.BlockSpec(memory_space=pltpu.SMEM)] + vmem(2),
        out_specs=tuple(vmem(2)),
        name="unpack",
        cost_estimate=pl.CostEstimate(flops=0, bytes_accessed=3 << 20, transcendentals=0),
    )(core, mine, other)


def exchange(blocks, axes):
    return lax.all_to_all(blocks, axes, split_axis=0, concat_axis=0, tiled=True)


def swap_cores(array):
    return lax.ppermute(array, "core", [(0, 1), (1, 0)])


def on_device(volume, cotangent, w_first, w_second):
    plane = ("z", "x")
    line = ("yl", "yh")
    core = lax.axis_index("core").astype(jnp.int32).reshape(1)
    cot = cotangent[0, 0]
    w2 = w_second.reshape(TAPS, 16, 256)
    packed = pack(volume, cot)
    got = shifted(packed, 1)
    cot_after, _ = lax.optimization_barrier((cot, packed))
    cot_hi = shifted(cot_after, -1)
    pre, gh, even, odd = early(volume, packed, cot, w_first, w2)
    gp, keep, send = middle(core, got, cot, cot_hi, pre, gh, even, odd, w_first, w2)
    upper = shifted(gp, -1)
    half = (keep + swap_cores(send).astype(F32)).astype(BF16)
    parts = exchange(half, plane)
    parts, upper = lax.optimization_barrier((parts, upper))
    mine = jnp.sum(parts.astype(F32), axis=0)
    lines = lax.axis_size(line)
    blocks = exchange(jnp.broadcast_to(mine[None], (lines,) + mine.shape), line)
    count = lax.axis_size(SAMPLE_AXES) * lax.axis_size(DEPTH_AXES) * 16 * 24
    scale = float(count) ** (-0.5)
    own_half = exchange(finish(blocks, lax.axis_size(plane), scale), plane)
    grad_input = input_backward(gp, upper, w_first)
    first, second = unpack(core, own_half, swap_cores(own_half))
    return (grad_input[None], first.reshape(3, 3, 3, 64, 128), second.reshape(3, 3, 3, 16, 256))


def solution(mesh):
    fine = Mesh(mesh.devices.reshape(2, 2, 8, 4, 4), SAMPLE_AXES + DEPTH_AXES)
    split = P(SAMPLE_AXES, DEPTH_AXES, None, None, None)
    return jax.shard_map(
        on_device,
        mesh=fine,
        in_specs=(split, split, P(), P()),
        out_specs=(split, P(), P()),
        check_vma=False,
    )
```

```python
import jax
import jax.numpy as jnp
from jax import lax
from jax.experimental import pallas as pl
from jax.experimental.pallas import tpu as pltpu
from jax.sharding import Mesh
from jax.sharding import PartitionSpec as P

GROUPS = 8
SAMPLE_AXES = ("yl", "core")
DEPTH_AXES = ("z", "x", "yh")
TAPS = 27
CHUNK = 48
PAD = 32
F32 = jnp.float32
BF16 = jnp.bfloat16

NT = (((1,), (1,)), ((), ()))
NN = (((1,), (0,)), ((), ()))
TN = (((0,), (0,)), ((), ()))


def dot(a, b, dims):
    return lax.dot_general(a, b, dims, preferred_element_type=F32)


def vmem(n):
    return [pl.BlockSpec(memory_space=pltpu.VMEM)] * n


def shifted(array, by):
    size = lax.axis_size(DEPTH_AXES)
    pairs = [(i, i + by) for i in range(size) if 0 <= i + by < size]
    return lax.ppermute(array, DEPTH_AXES, pairs)


def clear(ref):
    ref[...] = jnp.zeros_like(ref)


def roll_rows(x, by):
    return pltpu.roll(x, by % x.shape[0], 0)


def half_turn(x):
    return pltpu.roll(x, 64, x.ndim - 1)


def low_lanes(shape):
    return lax.broadcasted_iota(jnp.int32, shape, len(shape) - 1) < 64


def pair_rows(plane, out, tmp):
    step = tmp.shape[0]
    low = low_lanes((step, 24, 128))

    def body(i, carry):
        r = i * step
        tmp[:, :, 0:64] = plane[pl.ds(r, step)].astype(F32)
        even = tmp[:, pl.ds(0, 24, 2), :]
        odd = half_turn(tmp[:, pl.ds(1, 24, 2), :])
        out[pl.ds(r, step)] = jnp.where(low, even, odd).astype(BF16)
        return carry

    lax.fori_loop(0, plane.shape[0] // step, body, 0)


def pack_kernel(vol, cot, out, tmp):
    pair_rows(vol.at[0, 0], out.at[0, 0:8], tmp)
    out[0, 8:12] = cot[:, :, 0:128]
    out[0, 12:16] = cot[:, :, 128:256]


def pack(volume, cot):
    return pl.pallas_call(
        pack_kernel,
        grid=(4,),
        out_shape=jax.ShapeDtypeStruct((4, 16, 24, 128), BF16),
        in_specs=[
            pl.BlockSpec((1, 1, 8, 48, 64), lambda i: (0, 1, i, 0, 0)),
            pl.BlockSpec((4, 24, 256), lambda i: (i, 0, 0)),
        ],
        out_specs=pl.BlockSpec((1, 16, 24, 128), lambda i: (i, 0, 0, 0)),
        scratch_shapes=[pltpu.VMEM((8, 48, 128), F32)],
        name="pack",
        compiler_params=pltpu.CompilerParams(vmem_limit_bytes=4 << 20),
        cost_estimate=pl.CostEstimate(flops=0, bytes_accessed=2 << 20, transcendentals=0),
    )(volume, cot)


def split_rows(packed, even, odd):
    for r in range(16):
        even[r, 0:24] = packed[r // 4, 2 * (r % 4)]
        odd[r + 1, 0:24] = packed[r // 4, 2 * (r % 4) + 1]


def window(even, odd, kr):
    rows = even[...] if kr == 1 else odd[kr // 2 : kr // 2 + 16]
    return rows.reshape(16 * PAD, 128)


def strided_terms(windows, w1):
    zeros = jnp.zeros((64, 128), BF16)

    def weights(kd, kr):
        left = jnp.concatenate([w1[kd, kr, 1], w1[kd, kr, 2]], axis=0)
        right = jnp.concatenate([zeros, w1[kd, kr, 0]], axis=0)
        return jnp.concatenate([left, right], axis=1)

    total = None
    for i in range(0, len(windows), 2):
        pair = windows[i : i + 2]
        x = jnp.concatenate([p[2] for p in pair], axis=1) if len(pair) == 2 else pair[0][2]
        w = jnp.concatenate([weights(p[0], p[1]) for p in pair], axis=0)
        term = dot(x, w, NN)
        total = term if total is None else total + term
    return total[:, 0:128] + roll_rows(total[:, 128:256], 1)


def own_group():
    lane_group = lax.broadcasted_iota(jnp.int32, (128, 256), 1) // 32
    return lane_group == lax.broadcasted_iota(jnp.int32, (128, 256), 0) // 16


def put_weights(w2, kd, wd):
    own = own_group()
    for kr in range(3):
        for kc in range(3):
            spread = jnp.concatenate([w2[kd * 9 + kr * 3 + kc]] * GROUPS, axis=0)
            wd[kr, kc * 128 : kc * 128 + 128] = jnp.where(own, spread, 0.0).astype(BF16)


def cot_window(cpad, kr):
    return cpad[2 - kr : 18 - kr].reshape(16 * PAD, 256)


def grouped_terms(cpad, wd):
    total = None
    for kr in range(3):
        term = dot(cot_window(cpad, kr), wd[kr], NT)
        total = term if total is None else total + term
    return total


def join_columns(total):
    return roll_rows(total[:, 0:128], -1) + total[:, 128:256] + roll_rows(total[:, 256:384], 1)


def early_kernel(vol, packed, cot, w1, w2, pre, gh, even, odd, tmp, pairs, cpad, wd):
    clear(even)
    clear(odd)
    clear(cpad)
    for g in range(4):
        pair_rows(vol.at[0, 0, 8 * g : 8 * g + 8], pairs.at[g], tmp)
    split_rows(pairs, even.at[0], odd.at[0])
    split_rows(packed, even.at[1], odd.at[1])
    cpad[1:17, 0:24] = cot[...]
    windows = []
    for kd in (1, 2):
        for kr in range(3):
            windows.append((kd, kr, window(even.at[kd - 1], odd.at[kd - 1], kr)))
    pre[...] = strided_terms(windows, w1)
    put_weights(w2, 1, wd)
    gh[...] = join_columns(grouped_terms(cpad, wd))


def early(volume, packed, cot, w1, w2):
    whole = lambda *shape: pl.BlockSpec(shape, lambda i: (0,) * len(shape))
    return pl.pallas_call(
        early_kernel,
        grid=(1,),
        out_shape=(
            jax.ShapeDtypeStruct((16 * PAD, 128), F32),
            jax.ShapeDtypeStruct((16 * PAD, 128), F32),
            jax.ShapeDtypeStruct((2, 16, PAD, 128), BF16),
            jax.ShapeDtypeStruct((2, 17, PAD, 128), BF16),
        ),
        in_specs=[
            whole(1, 1, 32, 48, 64),
            whole(4, 16, 24, 128),
            whole(16, 24, 256),
            whole(3, 3, 3, 64, 128),
            whole(27, 16, 256),
        ],
        out_specs=(
            whole(16 * PAD, 128),
            whole(16 * PAD, 128),
            whole(2, 16, PAD, 128),
            whole(2, 17, PAD, 128),
        ),
        scratch_shapes=[
            pltpu.VMEM((8, 48, 128), F32),
            pltpu.VMEM((4, 8, 24, 128), BF16),
            pltpu.VMEM((18, PAD, 256), BF16),
            pltpu.VMEM((3, 384, 256), BF16),
        ],
        name="early",
        compiler_params=pltpu.CompilerParams(vmem_limit_bytes=12 << 20),
        cost_estimate=pl.CostEstimate(flops=1 << 30, bytes_accessed=2 << 20, transcendentals=0),
    )(volume, packed, cot, w1, w2)


def middle_kernel(
    core, got, cot_hi, cot, pre_part, gh_part, even12, odd12, w1, w2,
    gp_out, keep_out, send_out,
    even0, odd0, cpad, wd, hid, ups, hid_t, ups_t,
):
    cells = 16 * PAD
    clear(even0)
    clear(odd0)
    clear(cpad)
    cpad[1, 1:17, 0:24] = cot[...]
    put_weights(w2, 0, wd.at[0])
    put_weights(w2, 2, wd.at[1])
    split_rows(got, even0, odd0)
    for g in range(4):
        cpad[0, 1 + 4 * g : 5 + 4 * g, 0:24, 0:128] = got[g, 8:12]
        cpad[0, 1 + 4 * g : 5 + 4 * g, 0:24, 128:256] = got[g, 12:16]
    cpad[2, 1:17, 0:24] = cot_hi[...]
    total = grouped_terms(cpad.at[2], wd.at[0]) + grouped_terms(cpad.at[0], wd.at[1])
    gh = (join_columns(total) + gh_part[...]).astype(BF16).astype(F32)
    windows = [[window(even0, odd0, kr) for kr in range(3)]]
    for p in range(2):
        windows.append([window(even12.at[p], odd12.at[p], kr) for kr in range(3)])
    pre = strided_terms([(0, kr, windows[0][kr]) for kr in range(3)], w1) + pre_part[...]
    inside = (lax.broadcasted_iota(jnp.int32, (cells, 128), 0) & (PAD - 1)) < 24
    pre = jnp.where(inside, pre, 0.0)
    s = jax.nn.sigmoid(pre)
    hidden = (pre * s).astype(BF16).astype(F32)
    grad = gh * s * (1.0 + pre * (1.0 - s))
    grad = jnp.where(inside, grad, 0.0).astype(BF16).astype(F32)
    ups[:, 0:128] = grad.astype(BF16)
    ups[:, 128:256] = roll_rows(grad, -1).astype(BF16)
    hid[:, 0:128] = roll_rows(hidden, 1).astype(BF16)
    hid[:, 128:256] = hidden.astype(BF16)
    hid[:, 256:384] = roll_rows(hidden, -1).astype(BF16)
    gp_out[...] = ups[:, 0:128].reshape(16, PAD, 128)[:, 0:24]
    ups_t[...] = ups[...].T
    hid_t[...] = hid[...].T
    first_core = core[0] == 0

    def put(tap, row, half0, half1):
        size = half0.shape[0]
        keep_out[tap, row : row + size] = jnp.where(first_core, half0, half1).astype(BF16)
        send_out[tap, row : row + size] = jnp.where(first_core, half1, half0).astype(BF16)

    low = low_lanes((32, 128))
    flat = [windows[kd][kr] for kd in range(3) for kr in range(3)]
    for i in range(0, 9, 2):
        pair = flat[i : i + 2]
        x = jnp.concatenate(pair, axis=1) if len(pair) == 2 else pair[0]
        term = dot(ups_t[...], x, NN)
        for j in range(len(pair)):
            part = term[:, j * 128 : j * 128 + 128]
            tap = (i + j) * 3
            centre, side = [], []
            right = []
            for half in range(2):
                p = part[half * 64 : half * 64 + 32]
                q = part[half * 64 + 32 : half * 64 + 64]
                p1 = part[128 + half * 64 : 128 + half * 64 + 32]
                q1 = part[128 + half * 64 + 32 : 128 + half * 64 + 64]
                centre.append(jnp.where(low, p, half_turn(q)))
                right.append(jnp.where(low, half_turn(p), q))
                side.append(jnp.where(low, half_turn(p1), q1))
            put(tap, 0, *side)
            put(tap + 1, 0, *centre)
            put(tap + 2, 0, *right)
    own = own_group()
    for kd in range(3):
        for kr in range(3):
            term = dot(hid_t[...], cot_window(cpad.at[2 - kd], kr), NN)
            for kc in range(3):
                part = jnp.where(own, term[kc * 128 : kc * 128 + 128], 0.0)
                part = jnp.sum(part.reshape(GROUPS, 16, 256), axis=0)
                put((kd * 3 + kr) * 3 + kc, 32, part[:, 0:128], part[:, 128:256])
    keep_out[TAPS:32] = jnp.zeros((32 - TAPS, CHUNK, 128), BF16)
    send_out[TAPS:32] = jnp.zeros((32 - TAPS, CHUNK, 128), BF16)


def middle(core, got, cot_hi, cot, pre, gh, even, odd, w1, w2):
    return pl.pallas_call(
        middle_kernel,
        out_shape=(
            jax.ShapeDtypeStruct((16, 24, 128), BF16),
            jax.ShapeDtypeStruct((32, CHUNK, 128), BF16),
            jax.ShapeDtypeStruct((32, CHUNK, 128), BF16),
        ),
        in_specs=[pl.BlockSpec(memory_space=pltpu.SMEM)]
        + vmem(9),
        out_specs=tuple(vmem(3)),
        scratch_shapes=[
            pltpu.VMEM((16, PAD, 128), BF16),
            pltpu.VMEM((17, PAD, 128), BF16),
            pltpu.VMEM((3, 18, PAD, 256), BF16),
            pltpu.VMEM((2, 3, 384, 256), BF16),
            pltpu.VMEM((16 * PAD, 384), BF16),
            pltpu.VMEM((16 * PAD, 256), BF16),
            pltpu.VMEM((384, 16 * PAD), BF16),
            pltpu.VMEM((256, 16 * PAD), BF16),
        ],
        name="middle",
        compiler_params=pltpu.CompilerParams(vmem_limit_bytes=20 << 20),
        cost_estimate=pl.CostEstimate(flops=3 << 30, bytes_accessed=4 << 20, transcendentals=1 << 16),
    )(core, got, cot_hi, cot, pre, gh, even, odd, w1, w2)


def input_kernel(gp, upper, w1, out, pad, tmp):
    h2, w = gp.shape[0], gp.shape[1]
    cells = h2 * PAD
    clear(pad)
    pad[0, 0:h2, 0:w] = gp[...]
    pad[1, 0:h2, 0:w] = upper[...]
    zeros = jnp.zeros((64, 128), BF16)
    for par in range(2):
        depth = ((0, 1),) if par == 0 else ((0, 2), (1, 0))
        for row_par in range(2):
            rows = ((0, 1),) if row_par == 0 else ((0, 2), (1, 0))
            total = None
            for plane, kd in depth:
                for start, kr in rows:
                    x = pad[plane, start : start + h2].reshape(cells, 128)
                    weights = jnp.concatenate(
                        [w1[kd, kr, 1], w1[kd, kr, 2], zeros, w1[kd, kr, 0]], axis=0
                    )
                    term = dot(x, weights, NT)
                    total = term if total is None else total + term
            both = total[:, 0:128] + roll_rows(total[:, 128:256], -1)
            turned = pltpu.roll(both, 64, 1)
            both = both.reshape(h2, PAD, 128)
            turned = turned.reshape(h2, PAD, 128)
            for r in range(h2):
                tmp[r % 2, pl.ds(0, w, 2), :] = both[r, 0:w]
                tmp[r % 2, pl.ds(1, w, 2), :] = turned[r, 0:w]
                out[par, 2 * r + row_par] = tmp[r % 2, :, 0:64].astype(BF16)


def input_backward(gp, upper, w1):
    return pl.pallas_call(
        input_kernel,
        out_shape=jax.ShapeDtypeStruct((2, 32, 48, 64), BF16),
        in_specs=vmem(3),
        out_specs=pl.BlockSpec(memory_space=pltpu.VMEM),
        scratch_shapes=[
            pltpu.VMEM((2, 17, PAD, 128), BF16),
            pltpu.VMEM((2, 48, 128), F32),
        ],
        name="input_backward",
        compiler_params=pltpu.CompilerParams(vmem_limit_bytes=10 << 20),
        cost_estimate=pl.CostEstimate(flops=1 << 30, bytes_accessed=2 << 20, transcendentals=0),
    )(gp, upper, w1)


def unpack_kernel(core, mine, other, first, second):
    first_core = core[0] == 0
    low = low_lanes((32, 128))
    halves = []
    for tap in range(mine.shape[0]):
        a = mine[tap].astype(F32)
        b = other[tap].astype(F32)
        half0 = jnp.where(first_core, a, b)
        half1 = jnp.where(first_core, b, a)
        second[tap, :, 0:128] = half0[32:48]
        second[tap, :, 128:256] = half1[32:48]
        halves.append((half0[0:32], half1[0:32]))
    for tap in range(0, mine.shape[0], 2):
        last = min(tap + 1, mine.shape[0] - 1)
        rows = []
        for half in range(2):
            a, b = halves[tap][half], halves[last][half]
            rows.append(jnp.where(low, a, half_turn(b)))
            rows.append(jnp.where(low, half_turn(a), b))
        turned = jnp.concatenate(rows, axis=0).T
        first[tap] = turned[0:64]
        if last > tap:
            first[last] = turned[64:128]


def unpack(core, mine, other):
    step = 9
    halves = pl.BlockSpec((step, CHUNK, 128), lambda i: (i, 0, 0))
    return pl.pallas_call(
        unpack_kernel,
        grid=(TAPS // step,),
        out_shape=(
            jax.ShapeDtypeStruct((TAPS, 64, 128), F32),
            jax.ShapeDtypeStruct((TAPS, 16, 256), F32),
        ),
        in_specs=[pl.BlockSpec(memory_space=pltpu.SMEM), halves, halves],
        out_specs=(
            pl.BlockSpec((step, 64, 128), lambda i: (i, 0, 0)),
            pl.BlockSpec((step, 16, 256), lambda i: (i, 0, 0)),
        ),
        name="unpack",
        compiler_params=pltpu.CompilerParams(vmem_limit_bytes=8 << 20),
        cost_estimate=pl.CostEstimate(flops=0, bytes_accessed=3 << 20, transcendentals=0),
    )(core, mine, other)


def exchange(blocks, axes):
    return lax.all_to_all(blocks, axes, split_axis=0, concat_axis=0, tiled=True)


def repeated(block, axes):
    return jnp.broadcast_to(block[None], (lax.axis_size(axes),) + block.shape)


def added(a, b):
    return (a.astype(F32) + b.astype(F32)).astype(BF16)


def total(blocks):
    return jnp.sum(blocks.astype(F32), axis=0)


def swap_cores(array):
    return lax.ppermute(array, "core", [(0, 1), (1, 0)])


def on_device(volume, cotangent, w_first, w_second):
    plane = ("z", "x")
    line = ("yl", "yh")
    core = lax.axis_index("core").astype(jnp.int32).reshape(1)
    cot = cotangent[0, 0]
    w2 = w_second.reshape(TAPS, 16, 256)
    packed = pack(pltpu.with_memory_space_constraint(volume, pltpu.HBM), cot)
    got = shifted(packed, 1)
    cot_after, _ = lax.optimization_barrier((cot, packed))
    cot_hi = shifted(cot_after, -1)
    pre, gh, even, odd = early(volume, packed, cot, w_first, w2)
    gp, keep, send = middle(core, got, cot_hi, cot, pre, gh, even, odd, w_first, w2)
    upper = shifted(gp, -1)
    half = added(keep, swap_cores(send))
    mine = total(exchange(half, plane)).astype(BF16)
    blocks = exchange(repeated(mine, line), line)
    count = lax.axis_size(SAMPLE_AXES) * lax.axis_size(DEPTH_AXES) * 16 * 24
    scale = float(count) ** (-0.5)
    mine = (total(blocks) * scale).astype(BF16)
    own_half = exchange(repeated(mine, plane), plane)
    own_half, upper = lax.optimization_barrier((own_half, upper))
    grad_input = input_backward(gp, upper, w_first)
    first, second = unpack(core, own_half, swap_cores(own_half))
    return (grad_input[None], first.reshape(3, 3, 3, 64, 128), second.reshape(3, 3, 3, 16, 256))


def solution(mesh):
    fine = Mesh(mesh.devices.reshape(2, 2, 8, 4, 4), SAMPLE_AXES + DEPTH_AXES)
    split = P(SAMPLE_AXES, DEPTH_AXES, None, None, None)
    return jax.shard_map(
        on_device,
        mesh=fine,
        in_specs=(split, split, P(), P()),
        out_specs=(split, P(), P()),
        check_vma=False,
    )
```

```python
import functools

import jax
import jax.numpy as jnp
from jax import lax
from jax.experimental import pallas as pl
from jax.experimental.pallas import tpu as pltpu
from jax.sharding import Mesh
from jax.sharding import PartitionSpec as P

GROUPS = 8
SAMPLE_AXES = ("yl", "core")
DEPTH_AXES = ("z", "x", "yh")
TAPS = 27
CHUNK = 48
PAD = 32
F32 = jnp.float32
BF16 = jnp.bfloat16

NT = (((1,), (1,)), ((), ()))
NN = (((1,), (0,)), ((), ()))
TN = (((0,), (0,)), ((), ()))


def dot(a, b, dims):
    return lax.dot_general(a, b, dims, preferred_element_type=F32)


def vmem(n):
    return [pl.BlockSpec(memory_space=pltpu.VMEM)] * n


def shifted(array, by):
    size = lax.axis_size(DEPTH_AXES)
    pairs = [(i, i + by) for i in range(size) if 0 <= i + by < size]
    return lax.ppermute(array, DEPTH_AXES, pairs)


def clear(ref):
    ref[...] = jnp.zeros_like(ref)


def roll_rows(x, by):
    return pltpu.roll(x, by % x.shape[0], 0)


def half_turn(x):
    return pltpu.roll(x, 64, x.ndim - 1)


def low_lanes(shape):
    return lax.broadcasted_iota(jnp.int32, shape, len(shape) - 1) < 64


def pair_rows(plane, out, tmp):
    step = tmp.shape[0]
    low = low_lanes((step, 24, 128))

    def body(i, carry):
        r = i * step
        tmp[:, :, 0:64] = plane[pl.ds(r, step)].astype(F32)
        even = tmp[:, pl.ds(0, 24, 2), :]
        odd = half_turn(tmp[:, pl.ds(1, 24, 2), :])
        out[pl.ds(r, step)] = jnp.where(low, even, odd).astype(BF16)
        return carry

    lax.fori_loop(0, plane.shape[0] // step, body, 0)


def pack_kernel(vol, cot, out, tmp):
    pair_rows(vol.at[0, 0], out.at[0, 0:8], tmp)
    out[0, 8:12] = cot[:, :, 0:128]
    out[0, 12:16] = cot[:, :, 128:256]


def pack(volume, cot):
    return pl.pallas_call(
        pack_kernel,
        grid=(4,),
        out_shape=jax.ShapeDtypeStruct((4, 16, 24, 128), BF16),
        in_specs=[
            pl.BlockSpec((1, 1, 8, 48, 64), lambda i: (0, 1, i, 0, 0)),
            pl.BlockSpec((4, 24, 256), lambda i: (i, 0, 0)),
        ],
        out_specs=pl.BlockSpec((1, 16, 24, 128), lambda i: (i, 0, 0, 0)),
        scratch_shapes=[pltpu.VMEM((8, 48, 128), F32)],
        name="pack",
        compiler_params=pltpu.CompilerParams(vmem_limit_bytes=4 << 20),
        cost_estimate=pl.CostEstimate(flops=0, bytes_accessed=2 << 20, transcendentals=0),
    )(volume, cot)


def split_rows(packed, even, odd):
    for r in range(16):
        even[r, 0:24] = packed[r // 4, 2 * (r % 4)]
        odd[r + 1, 0:24] = packed[r // 4, 2 * (r % 4) + 1]


def window(even, odd, kr):
    rows = even[...] if kr == 1 else odd[kr // 2 : kr // 2 + 16]
    return rows.reshape(16 * PAD, 128)


def strided_terms(windows, w1):
    zeros = jnp.zeros((64, 128), BF16)

    def weights(kd, kr):
        left = jnp.concatenate([w1[kd, kr, 1], w1[kd, kr, 2]], axis=0)
        right = jnp.concatenate([zeros, w1[kd, kr, 0]], axis=0)
        return jnp.concatenate([left, right], axis=1)

    total = None
    for i in range(0, len(windows), 2):
        pair = windows[i : i + 2]
        x = jnp.concatenate([p[2] for p in pair], axis=1) if len(pair) == 2 else pair[0][2]
        w = jnp.concatenate([weights(p[0], p[1]) for p in pair], axis=0)
        term = dot(x, w, NN)
        total = term if total is None else total + term
    return total[:, 0:128] + roll_rows(total[:, 128:256], 1)


def own_group():
    lane_group = lax.broadcasted_iota(jnp.int32, (128, 256), 1) // 32
    return lane_group == lax.broadcasted_iota(jnp.int32, (128, 256), 0) // 16


def put_weights(w2, kd, wd):
    own = own_group()
    for kr in range(3):
        for kc in range(3):
            spread = jnp.concatenate([w2[kd * 9 + kr * 3 + kc]] * GROUPS, axis=0)
            wd[kr, kc * 128 : kc * 128 + 128] = jnp.where(own, spread, 0.0).astype(BF16)


def cot_window(cpad, kr):
    return cpad[2 - kr : 18 - kr].reshape(16 * PAD, 256)


def grouped_terms(cpad, wd):
    total = None
    for kr in range(3):
        term = dot(cot_window(cpad, kr), wd[kr], NT)
        total = term if total is None else total + term
    return total


def join_columns(total):
    return roll_rows(total[:, 0:128], -1) + total[:, 128:256] + roll_rows(total[:, 256:384], 1)


def early_kernel(vol, packed, cot, w1, w2, pre, gh, even, odd, wd02, tmp, pairs, cpad, wd):
    clear(even)
    clear(odd)
    clear(cpad)
    for g in range(4):
        pair_rows(vol.at[0, 0, 8 * g : 8 * g + 8], pairs.at[g], tmp)
    split_rows(pairs, even.at[0], odd.at[0])
    split_rows(packed, even.at[1], odd.at[1])
    cpad[1:17, 0:24] = cot[...]
    windows = []
    for kd in (1, 2):
        for kr in range(3):
            windows.append((kd, kr, window(even.at[kd - 1], odd.at[kd - 1], kr)))
    pre[...] = strided_terms(windows, w1)
    put_weights(w2, 1, wd)
    gh[...] = join_columns(grouped_terms(cpad, wd))
    put_weights(w2, 0, wd02.at[0])
    put_weights(w2, 2, wd02.at[1])


def early(volume, packed, cot, w1, w2):
    whole = lambda *shape: pl.BlockSpec(shape, lambda i: (0,) * len(shape))
    return pl.pallas_call(
        early_kernel,
        grid=(1,),
        out_shape=(
            jax.ShapeDtypeStruct((16 * PAD, 128), F32),
            jax.ShapeDtypeStruct((16 * PAD, 128), F32),
            jax.ShapeDtypeStruct((2, 16, PAD, 128), BF16),
            jax.ShapeDtypeStruct((2, 17, PAD, 128), BF16),
            jax.ShapeDtypeStruct((2, 3, 384, 256), BF16),
        ),
        in_specs=[
            whole(1, 1, 32, 48, 64),
            whole(4, 16, 24, 128),
            whole(16, 24, 256),
            whole(3, 3, 3, 64, 128),
            whole(27, 16, 256),
        ],
        out_specs=(
            whole(16 * PAD, 128),
            whole(16 * PAD, 128),
            whole(2, 16, PAD, 128),
            whole(2, 17, PAD, 128),
            whole(2, 3, 384, 256),
        ),
        scratch_shapes=[
            pltpu.VMEM((8, 48, 128), F32),
            pltpu.VMEM((4, 8, 24, 128), BF16),
            pltpu.VMEM((18, PAD, 256), BF16),
            pltpu.VMEM((3, 384, 256), BF16),
        ],
        name="early",
        compiler_params=pltpu.CompilerParams(vmem_limit_bytes=12 << 20),
        cost_estimate=pl.CostEstimate(flops=1 << 30, bytes_accessed=2 << 20, transcendentals=0),
    )(volume, packed, cot, w1, w2)


def upper_kernel(cot_hi, gh_part, wd, gh, cpad):
    clear(cpad)
    cpad[1:17, 0:24] = cot_hi[...]
    gh[...] = gh_part[...] + join_columns(grouped_terms(cpad, wd.at[0]))


def upper_share(cot_hi, gh, wd):
    return pl.pallas_call(
        upper_kernel,
        out_shape=(
            jax.ShapeDtypeStruct((16 * PAD, 128), F32),
            jax.ShapeDtypeStruct((18, PAD, 256), BF16),
        ),
        in_specs=vmem(3),
        out_specs=tuple(vmem(2)),
        name="upper_share",
        compiler_params=pltpu.CompilerParams(vmem_limit_bytes=8 << 20),
        cost_estimate=pl.CostEstimate(flops=1 << 29, bytes_accessed=2 << 20, transcendentals=0),
    )(cot_hi, gh, wd)


def middle_kernel(
    core, got, cpad_hi, cot, pre_part, gh_part, even12, odd12, w1, wd,
    gp_out, keep_out, send_out,
    even0, odd0, cpad, hid, ups, hid_t, ups_t,
):
    cells = 16 * PAD
    clear(even0)
    clear(odd0)
    clear(cpad)
    cpad[1, 1:17, 0:24] = cot[...]
    split_rows(got, even0, odd0)
    for g in range(4):
        cpad[0, 1 + 4 * g : 5 + 4 * g, 0:24, 0:128] = got[g, 8:12]
        cpad[0, 1 + 4 * g : 5 + 4 * g, 0:24, 128:256] = got[g, 12:16]
    total = grouped_terms(cpad.at[0], wd.at[1])
    planes = (cpad_hi, cpad.at[1], cpad.at[0])
    gh = (join_columns(total) + gh_part[...]).astype(BF16).astype(F32)
    windows = [[window(even0, odd0, kr) for kr in range(3)]]
    for p in range(2):
        windows.append([window(even12.at[p], odd12.at[p], kr) for kr in range(3)])
    pre = strided_terms([(0, kr, windows[0][kr]) for kr in range(3)], w1) + pre_part[...]
    inside = (lax.broadcasted_iota(jnp.int32, (cells, 128), 0) & (PAD - 1)) < 24
    pre = jnp.where(inside, pre, 0.0)
    s = jax.nn.sigmoid(pre)
    hidden = (pre * s).astype(BF16).astype(F32)
    grad = gh * s * (1.0 + pre * (1.0 - s))
    grad = jnp.where(inside, grad, 0.0).astype(BF16).astype(F32)
    ups[:, 0:128] = grad.astype(BF16)
    ups[:, 128:256] = roll_rows(grad, -1).astype(BF16)
    hid[:, 0:128] = roll_rows(hidden, 1).astype(BF16)
    hid[:, 128:256] = hidden.astype(BF16)
    hid[:, 256:384] = roll_rows(hidden, -1).astype(BF16)
    gp_out[...] = ups[:, 0:128].reshape(16, PAD, 128)[:, 0:24]
    ups_t[...] = ups[...].T
    hid_t[...] = hid[...].T
    first_core = core[0] == 0

    def put(tap, row, half0, half1):
        size = half0.shape[0]
        keep_out[tap, row : row + size] = jnp.where(first_core, half0, half1).astype(BF16)
        send_out[tap, row : row + size] = jnp.where(first_core, half1, half0).astype(BF16)

    low = low_lanes((32, 128))
    flat = [windows[kd][kr] for kd in range(3) for kr in range(3)]
    for i in range(0, 9, 2):
        pair = flat[i : i + 2]
        x = jnp.concatenate(pair, axis=1) if len(pair) == 2 else pair[0]
        term = dot(ups_t[...], x, NN)
        for j in range(len(pair)):
            part = term[:, j * 128 : j * 128 + 128]
            tap = (i + j) * 3
            centre, side = [], []
            right = []
            for half in range(2):
                p = part[half * 64 : half * 64 + 32]
                q = part[half * 64 + 32 : half * 64 + 64]
                p1 = part[128 + half * 64 : 128 + half * 64 + 32]
                q1 = part[128 + half * 64 + 32 : 128 + half * 64 + 64]
                centre.append(jnp.where(low, p, half_turn(q)))
                right.append(jnp.where(low, half_turn(p), q))
                side.append(jnp.where(low, half_turn(p1), q1))
            put(tap, 0, *side)
            put(tap + 1, 0, *centre)
            put(tap + 2, 0, *right)
    own = own_group()
    for kd in range(3):
        for kr in range(3):
            term = dot(hid_t[...], cot_window(planes[kd], kr), NN)
            for kc in range(3):
                part = jnp.where(own, term[kc * 128 : kc * 128 + 128], 0.0)
                part = jnp.sum(part.reshape(GROUPS, 16, 256), axis=0)
                put((kd * 3 + kr) * 3 + kc, 32, part[:, 0:128], part[:, 128:256])
    keep_out[TAPS:32] = jnp.zeros((32 - TAPS, CHUNK, 128), BF16)
    send_out[TAPS:32] = jnp.zeros((32 - TAPS, CHUNK, 128), BF16)


def middle(core, got, cpad_hi, cot, pre, gh, even, odd, w1, wd):
    return pl.pallas_call(
        middle_kernel,
        out_shape=(
            jax.ShapeDtypeStruct((16, 24, 128), BF16),
            jax.ShapeDtypeStruct((32, CHUNK, 128), BF16),
            jax.ShapeDtypeStruct((32, CHUNK, 128), BF16),
        ),
        in_specs=[pl.BlockSpec(memory_space=pltpu.SMEM)]
        + vmem(9),
        out_specs=tuple(vmem(3)),
        scratch_shapes=[
            pltpu.VMEM((16, PAD, 128), BF16),
            pltpu.VMEM((17, PAD, 128), BF16),
            pltpu.VMEM((2, 18, PAD, 256), BF16),
            pltpu.VMEM((16 * PAD, 384), BF16),
            pltpu.VMEM((16 * PAD, 256), BF16),
            pltpu.VMEM((384, 16 * PAD), BF16),
            pltpu.VMEM((256, 16 * PAD), BF16),
        ],
        name="middle",
        compiler_params=pltpu.CompilerParams(vmem_limit_bytes=20 << 20),
        cost_estimate=pl.CostEstimate(flops=3 << 30, bytes_accessed=4 << 20, transcendentals=1 << 16),
    )(core, got, cpad_hi, cot, pre, gh, even, odd, w1, wd)


def input_kernel(gp, upper, w1, out, pad, tmp):
    h2, w = gp.shape[0], gp.shape[1]
    cells = h2 * PAD
    clear(pad)
    pad[0, 0:h2, 0:w] = gp[...]
    pad[1, 0:h2, 0:w] = upper[...]
    zeros = jnp.zeros((64, 128), BF16)
    for par in range(2):
        depth = ((0, 1),) if par == 0 else ((0, 2), (1, 0))
        for row_par in range(2):
            rows = ((0, 1),) if row_par == 0 else ((0, 2), (1, 0))
            total = None
            for plane, kd in depth:
                for start, kr in rows:
                    x = pad[plane, start : start + h2].reshape(cells, 128)
                    weights = jnp.concatenate(
                        [w1[kd, kr, 1], w1[kd, kr, 2], zeros, w1[kd, kr, 0]], axis=0
                    )
                    term = dot(x, weights, NT)
                    total = term if total is None else total + term
            both = total[:, 0:128] + roll_rows(total[:, 128:256], -1)
            turned = pltpu.roll(both, 64, 1)
            both = both.reshape(h2, PAD, 128)
            turned = turned.reshape(h2, PAD, 128)
            for r in range(h2):
                tmp[r % 2, pl.ds(0, w, 2), :] = both[r, 0:w]
                tmp[r % 2, pl.ds(1, w, 2), :] = turned[r, 0:w]
                out[par, 2 * r + row_par] = tmp[r % 2, :, 0:64].astype(BF16)


def input_backward(gp, upper, w1):
    return pl.pallas_call(
        input_kernel,
        out_shape=jax.ShapeDtypeStruct((2, 32, 48, 64), BF16),
        in_specs=vmem(3),
        out_specs=pl.BlockSpec(memory_space=pltpu.VMEM),
        scratch_shapes=[
            pltpu.VMEM((2, 17, PAD, 128), BF16),
            pltpu.VMEM((2, 48, 128), F32),
        ],
        name="input_backward",
        compiler_params=pltpu.CompilerParams(vmem_limit_bytes=10 << 20),
        cost_estimate=pl.CostEstimate(flops=1 << 30, bytes_accessed=2 << 20, transcendentals=0),
    )(gp, upper, w1)


def finish_kernel(scale, blocks, out):
    total = jnp.sum(blocks[...].astype(F32), axis=0) * scale
    packed = total[0:32]
    flipped = packed.T
    turned = jnp.concatenate([flipped[0:64], flipped[64:128]], axis=1)
    top = jnp.concatenate([turned[0:32], turned[32:64]], axis=1)
    mine = jnp.concatenate([top, total[32:48]], axis=0).astype(BF16)
    out[...] = jnp.broadcast_to(mine[None], out.shape)


def finish(blocks, count, scale):
    return pl.pallas_call(
        functools.partial(finish_kernel, scale),
        out_shape=jax.ShapeDtypeStruct((count, CHUNK, 128), BF16),
        in_specs=vmem(1),
        out_specs=pl.BlockSpec(memory_space=pltpu.VMEM),
        name="finish",
        compiler_params=pltpu.CompilerParams(vmem_limit_bytes=4 << 20),
        cost_estimate=pl.CostEstimate(flops=1 << 16, bytes_accessed=1 << 20, transcendentals=0),
    )(blocks)


def unpack_kernel(core, mine, other, first, second):
    first_core = core[0] == 0
    low = low_lanes((32, 128))
    for tap in range(mine.shape[0]):
        a = mine[tap].astype(F32)
        b = other[tap].astype(F32)
        half0 = jnp.where(first_core, a, b)
        half1 = jnp.where(first_core, b, a)
        top, bottom = half0[0:32], half1[0:32]
        first[tap, 0:32] = jnp.where(low, top, half_turn(bottom))
        first[tap, 32:64] = jnp.where(low, half_turn(top), bottom)
        second[tap, :, 0:128] = half0[32:48]
        second[tap, :, 128:256] = half1[32:48]


def unpack(core, mine, other):
    step = 9
    halves = pl.BlockSpec((step, CHUNK, 128), lambda i: (i, 0, 0))
    return pl.pallas_call(
        unpack_kernel,
        grid=(TAPS // step,),
        out_shape=(
            jax.ShapeDtypeStruct((TAPS, 64, 128), F32),
            jax.ShapeDtypeStruct((TAPS, 16, 256), F32),
        ),
        in_specs=[pl.BlockSpec(memory_space=pltpu.SMEM), halves, halves],
        out_specs=(
            pl.BlockSpec((step, 64, 128), lambda i: (i, 0, 0)),
            pl.BlockSpec((step, 16, 256), lambda i: (i, 0, 0)),
        ),
        name="unpack",
        compiler_params=pltpu.CompilerParams(vmem_limit_bytes=8 << 20),
        cost_estimate=pl.CostEstimate(flops=0, bytes_accessed=3 << 20, transcendentals=0),
    )(core, mine, other)


def exchange(blocks, axes):
    return lax.all_to_all(blocks, axes, split_axis=0, concat_axis=0, tiled=True)


def repeated(block, axes):
    return jnp.broadcast_to(block[None], (lax.axis_size(axes),) + block.shape)


def added(a, b):
    return (a.astype(F32) + b.astype(F32)).astype(BF16)


def total(blocks):
    return jnp.sum(blocks.astype(F32), axis=0)


def swap_cores(array):
    return lax.ppermute(array, "core", [(0, 1), (1, 0)])


def on_device(volume, cotangent, w_first, w_second):
    plane = ("z", "x")
    line = ("yl", "yh")
    core = lax.axis_index("core").astype(jnp.int32).reshape(1)
    cot = cotangent[0, 0]
    w2 = w_second.reshape(TAPS, 16, 256)
    packed = pack(pltpu.with_memory_space_constraint(volume, pltpu.HBM), cot)
    got = shifted(packed, 1)
    cot_after, _ = lax.optimization_barrier((cot, packed))
    cot_hi = shifted(cot_after, -1)
    pre, gh, even, odd, wd = early(volume, packed, cot, w_first, w2)
    gh, cpad_hi = upper_share(cot_hi, gh, wd)
    gp, keep, send = middle(core, got, cpad_hi, cot, pre, gh, even, odd, w_first, wd)
    upper = shifted(gp, -1)
    half = added(keep, swap_cores(send))
    mine = total(exchange(half, plane)).astype(BF16)
    blocks = exchange(repeated(mine, line), line)
    count = lax.axis_size(SAMPLE_AXES) * lax.axis_size(DEPTH_AXES) * 16 * 24
    scale = float(count) ** (-0.5)
    own_half = exchange(finish(blocks, lax.axis_size(plane), scale), plane)
    own_half, upper = lax.optimization_barrier((own_half, upper))
    grad_input = input_backward(gp, upper, w_first)
    first, second = unpack(core, own_half, swap_cores(own_half))
    return (grad_input[None], first.reshape(3, 3, 3, 64, 128), second.reshape(3, 3, 3, 16, 256))


def solution(mesh):
    fine = Mesh(mesh.devices.reshape(2, 2, 8, 4, 4), SAMPLE_AXES + DEPTH_AXES)
    split = P(SAMPLE_AXES, DEPTH_AXES, None, None, None)
    return jax.shard_map(
        on_device,
        mesh=fine,
        in_specs=(split, split, P(), P()),
        out_specs=(split, P(), P()),
        check_vma=False,
    )
```

```python
import functools

import jax
import jax.numpy as jnp
from jax import lax
from jax.experimental import pallas as pl
from jax.experimental.pallas import tpu as pltpu
from jax.sharding import Mesh
from jax.sharding import PartitionSpec as P

GROUPS = 8
SAMPLE_AXES = ("yl", "core")
DEPTH_AXES = ("z", "x", "yh")
TAPS = 27
CHUNK = 48
PAD = 32
F32 = jnp.float32
BF16 = jnp.bfloat16

NT = (((1,), (1,)), ((), ()))
NN = (((1,), (0,)), ((), ()))
TN = (((0,), (0,)), ((), ()))


def dot(a, b, dims):
    return lax.dot_general(a, b, dims, preferred_element_type=F32)


def vmem(n):
    return [pl.BlockSpec(memory_space=pltpu.VMEM)] * n


def shifted(array, by):
    size = lax.axis_size(DEPTH_AXES)
    pairs = [(i, i + by) for i in range(size) if 0 <= i + by < size]
    return lax.ppermute(array, DEPTH_AXES, pairs)


def clear(ref):
    ref[...] = jnp.zeros_like(ref)


def roll_rows(x, by):
    return pltpu.roll(x, by % x.shape[0], 0)


def half_turn(x):
    return pltpu.roll(x, 64, x.ndim - 1)


def low_lanes(shape):
    return lax.broadcasted_iota(jnp.int32, shape, len(shape) - 1) < 64


def pair_rows(plane, out, tmp):
    step = tmp.shape[0]
    low = low_lanes((step, 24, 128))

    def body(i, carry):
        r = i * step
        tmp[:, :, 0:64] = plane[pl.ds(r, step)].astype(F32)
        even = tmp[:, pl.ds(0, 24, 2), :]
        odd = half_turn(tmp[:, pl.ds(1, 24, 2), :])
        out[pl.ds(r, step)] = jnp.where(low, even, odd).astype(BF16)
        return carry

    lax.fori_loop(0, plane.shape[0] // step, body, 0)


def pack_kernel(vol, cot, out, tmp):
    pair_rows(vol.at[0, 0], out.at[0, 0:8], tmp)
    out[0, 8:12] = cot[:, :, 0:128]
    out[0, 12:16] = cot[:, :, 128:256]


def pack(volume, cot):
    return pl.pallas_call(
        pack_kernel,
        grid=(4,),
        out_shape=jax.ShapeDtypeStruct((4, 16, 24, 128), BF16),
        in_specs=[
            pl.BlockSpec((1, 1, 8, 48, 64), lambda i: (0, 1, i, 0, 0)),
            pl.BlockSpec((4, 24, 256), lambda i: (i, 0, 0)),
        ],
        out_specs=pl.BlockSpec((1, 16, 24, 128), lambda i: (i, 0, 0, 0)),
        scratch_shapes=[pltpu.VMEM((8, 48, 128), F32)],
        name="pack",
        compiler_params=pltpu.CompilerParams(vmem_limit_bytes=4 << 20),
        cost_estimate=pl.CostEstimate(flops=0, bytes_accessed=2 << 20, transcendentals=0),
    )(volume, cot)


def split_rows(packed, even, odd):
    for r in range(16):
        even[r, 0:24] = packed[r // 4, 2 * (r % 4)]
        odd[r + 1, 0:24] = packed[r // 4, 2 * (r % 4) + 1]


def window(even, odd, kr):
    rows = even[...] if kr == 1 else odd[kr // 2 : kr // 2 + 16]
    return rows.reshape(16 * PAD, 128)


def strided_terms(windows, w1):
    zeros = jnp.zeros((64, 128), BF16)

    def weights(kd, kr):
        left = jnp.concatenate([w1[kd, kr, 1], w1[kd, kr, 2]], axis=0)
        right = jnp.concatenate([zeros, w1[kd, kr, 0]], axis=0)
        return jnp.concatenate([left, right], axis=1)

    total = None
    for i in range(0, len(windows), 2):
        pair = windows[i : i + 2]
        x = jnp.concatenate([p[2] for p in pair], axis=1) if len(pair) == 2 else pair[0][2]
        w = jnp.concatenate([weights(p[0], p[1]) for p in pair], axis=0)
        term = dot(x, w, NN)
        total = term if total is None else total + term
    return total[:, 0:128] + roll_rows(total[:, 128:256], 1)


def own_group():
    lane_group = lax.broadcasted_iota(jnp.int32, (128, 256), 1) // 32
    return lane_group == lax.broadcasted_iota(jnp.int32, (128, 256), 0) // 16


def put_weights(w2, kd, wd):
    own = own_group()
    for kr in range(3):
        for kc in range(3):
            spread = jnp.concatenate([w2[kd * 9 + kr * 3 + kc]] * GROUPS, axis=0)
            wd[kr, kc * 128 : kc * 128 + 128] = jnp.where(own, spread, 0.0).astype(BF16)


def cot_window(cpad, kr):
    return cpad[2 - kr : 18 - kr].reshape(16 * PAD, 256)


def grouped_terms(cpad, wd):
    total = None
    for kr in range(3):
        term = dot(cot_window(cpad, kr), wd[kr], NT)
        total = term if total is None else total + term
    return total


def join_columns(total):
    return roll_rows(total[:, 0:128], -1) + total[:, 128:256] + roll_rows(total[:, 256:384], 1)


def early_kernel(vol, packed, cot, w1, w2, pre, gh, even, odd, wd02, tmp, pairs, cpad, wd):
    clear(even)
    clear(odd)
    clear(cpad)
    for g in range(4):
        pair_rows(vol.at[0, 0, 8 * g : 8 * g + 8], pairs.at[g], tmp)
    split_rows(pairs, even.at[0], odd.at[0])
    split_rows(packed, even.at[1], odd.at[1])
    cpad[1:17, 0:24] = cot[...]
    windows = []
    for kd in (1, 2):
        for kr in range(3):
            windows.append((kd, kr, window(even.at[kd - 1], odd.at[kd - 1], kr)))
    pre[...] = strided_terms(windows, w1)
    put_weights(w2, 1, wd)
    gh[...] = join_columns(grouped_terms(cpad, wd))
    put_weights(w2, 0, wd02.at[0])
    put_weights(w2, 2, wd02.at[1])


def early(volume, packed, cot, w1, w2):
    whole = lambda *shape: pl.BlockSpec(shape, lambda i: (0,) * len(shape))
    return pl.pallas_call(
        early_kernel,
        grid=(1,),
        out_shape=(
            jax.ShapeDtypeStruct((16 * PAD, 128), F32),
            jax.ShapeDtypeStruct((16 * PAD, 128), F32),
            jax.ShapeDtypeStruct((2, 16, PAD, 128), BF16),
            jax.ShapeDtypeStruct((2, 17, PAD, 128), BF16),
            jax.ShapeDtypeStruct((2, 3, 384, 256), BF16),
        ),
        in_specs=[
            whole(1, 1, 32, 48, 64),
            whole(4, 16, 24, 128),
            whole(16, 24, 256),
            whole(3, 3, 3, 64, 128),
            whole(27, 16, 256),
        ],
        out_specs=(
            whole(16 * PAD, 128),
            whole(16 * PAD, 128),
            whole(2, 16, PAD, 128),
            whole(2, 17, PAD, 128),
            whole(2, 3, 384, 256),
        ),
        scratch_shapes=[
            pltpu.VMEM((8, 48, 128), F32),
            pltpu.VMEM((4, 8, 24, 128), BF16),
            pltpu.VMEM((18, PAD, 256), BF16),
            pltpu.VMEM((3, 384, 256), BF16),
        ],
        name="early",
        compiler_params=pltpu.CompilerParams(vmem_limit_bytes=12 << 20),
        cost_estimate=pl.CostEstimate(flops=1 << 30, bytes_accessed=2 << 20, transcendentals=0),
    )(volume, packed, cot, w1, w2)


def upper_kernel(cot_hi, gh_part, wd, gh, cpad):
    clear(cpad)
    cpad[1:17, 0:24] = cot_hi[...]
    gh[...] = gh_part[...] + join_columns(grouped_terms(cpad, wd.at[0]))


def upper_share(cot_hi, gh, wd):
    return pl.pallas_call(
        upper_kernel,
        out_shape=(
            jax.ShapeDtypeStruct((16 * PAD, 128), F32),
            jax.ShapeDtypeStruct((18, PAD, 256), BF16),
        ),
        in_specs=vmem(3),
        out_specs=tuple(vmem(2)),
        name="upper_share",
        compiler_params=pltpu.CompilerParams(vmem_limit_bytes=8 << 20),
        cost_estimate=pl.CostEstimate(flops=1 << 29, bytes_accessed=2 << 20, transcendentals=0),
    )(cot_hi, gh, wd)


def middle_kernel(
    core, got, cpad_hi, cot, pre_part, gh_part, even12, odd12, w1, wd,
    gp_out, keep_out, send_out,
    even0, odd0, cpad, hid, ups, hid_t, ups_t,
):
    cells = 16 * PAD
    clear(even0)
    clear(odd0)
    clear(cpad)
    cpad[1, 1:17, 0:24] = cot[...]
    split_rows(got, even0, odd0)
    for g in range(4):
        cpad[0, 1 + 4 * g : 5 + 4 * g, 0:24, 0:128] = got[g, 8:12]
        cpad[0, 1 + 4 * g : 5 + 4 * g, 0:24, 128:256] = got[g, 12:16]
    total = grouped_terms(cpad.at[0], wd.at[1])
    planes = (cpad_hi, cpad.at[1], cpad.at[0])
    gh = (join_columns(total) + gh_part[...]).astype(BF16).astype(F32)
    windows = [[window(even0, odd0, kr) for kr in range(3)]]
    for p in range(2):
        windows.append([window(even12.at[p], odd12.at[p], kr) for kr in range(3)])
    pre = strided_terms([(0, kr, windows[0][kr]) for kr in range(3)], w1) + pre_part[...]
    inside = (lax.broadcasted_iota(jnp.int32, (cells, 128), 0) & (PAD - 1)) < 24
    pre = jnp.where(inside, pre, 0.0)
    s = jax.nn.sigmoid(pre)
    hidden = (pre * s).astype(BF16).astype(F32)
    grad = gh * s * (1.0 + pre * (1.0 - s))
    grad = jnp.where(inside, grad, 0.0).astype(BF16).astype(F32)
    ups[:, 0:128] = grad.astype(BF16)
    ups[:, 128:256] = roll_rows(grad, -1).astype(BF16)
    hid[:, 0:128] = roll_rows(hidden, 1).astype(BF16)
    hid[:, 128:256] = hidden.astype(BF16)
    hid[:, 256:384] = roll_rows(hidden, -1).astype(BF16)
    gp_out[...] = ups[:, 0:128].reshape(16, PAD, 128)[:, 0:24]
    ups_t[...] = ups[...].T
    hid_t[...] = hid[...].T
    first_core = core[0] == 0

    def put(tap, row, half0, half1):
        size = half0.shape[0]
        keep_out[tap, row : row + size] = jnp.where(first_core, half0, half1).astype(BF16)
        send_out[tap, row : row + size] = jnp.where(first_core, half1, half0).astype(BF16)

    low = low_lanes((32, 128))
    flat = [windows[kd][kr] for kd in range(3) for kr in range(3)]
    for i in range(0, 9, 2):
        pair = flat[i : i + 2]
        x = jnp.concatenate(pair, axis=1) if len(pair) == 2 else pair[0]
        term = dot(ups_t[...], x, NN)
        for j in range(len(pair)):
            part = term[:, j * 128 : j * 128 + 128]
            tap = (i + j) * 3
            centre, side = [], []
            right = []
            for half in range(2):
                p = part[half * 64 : half * 64 + 32]
                q = part[half * 64 + 32 : half * 64 + 64]
                p1 = part[128 + half * 64 : 128 + half * 64 + 32]
                q1 = part[128 + half * 64 + 32 : 128 + half * 64 + 64]
                centre.append(jnp.where(low, p, half_turn(q)))
                right.append(jnp.where(low, half_turn(p), q))
                side.append(jnp.where(low, half_turn(p1), q1))
            put(tap, 0, *side)
            put(tap + 1, 0, *centre)
            put(tap + 2, 0, *right)
    own = own_group()
    for kd in range(3):
        for kr in range(3):
            term = dot(hid_t[...], cot_window(planes[kd], kr), NN)
            for kc in range(3):
                part = jnp.where(own, term[kc * 128 : kc * 128 + 128], 0.0)
                part = jnp.sum(part.reshape(GROUPS, 16, 256), axis=0)
                put((kd * 3 + kr) * 3 + kc, 32, part[:, 0:128], part[:, 128:256])
    keep_out[TAPS:32] = jnp.zeros((32 - TAPS, CHUNK, 128), BF16)
    send_out[TAPS:32] = jnp.zeros((32 - TAPS, CHUNK, 128), BF16)


def middle(core, got, cpad_hi, cot, pre, gh, even, odd, w1, wd):
    return pl.pallas_call(
        middle_kernel,
        out_shape=(
            jax.ShapeDtypeStruct((16, 24, 128), BF16),
            jax.ShapeDtypeStruct((32, CHUNK, 128), BF16),
            jax.ShapeDtypeStruct((32, CHUNK, 128), BF16),
        ),
        in_specs=[pl.BlockSpec(memory_space=pltpu.SMEM)]
        + vmem(9),
        out_specs=tuple(vmem(3)),
        scratch_shapes=[
            pltpu.VMEM((16, PAD, 128), BF16),
            pltpu.VMEM((17, PAD, 128), BF16),
            pltpu.VMEM((2, 18, PAD, 256), BF16),
            pltpu.VMEM((16 * PAD, 384), BF16),
            pltpu.VMEM((16 * PAD, 256), BF16),
            pltpu.VMEM((384, 16 * PAD), BF16),
            pltpu.VMEM((256, 16 * PAD), BF16),
        ],
        name="middle",
        compiler_params=pltpu.CompilerParams(vmem_limit_bytes=20 << 20),
        cost_estimate=pl.CostEstimate(flops=3 << 30, bytes_accessed=4 << 20, transcendentals=1 << 16),
    )(core, got, cpad_hi, cot, pre, gh, even, odd, w1, wd)


def input_kernel(gp, upper, w1, out, pad, tmp):
    h2, w = gp.shape[0], gp.shape[1]
    cells = h2 * PAD
    clear(pad)
    pad[0, 0:h2, 0:w] = gp[...]
    pad[1, 0:h2, 0:w] = upper[...]
    zeros = jnp.zeros((64, 128), BF16)
    for par in range(2):
        depth = ((0, 1),) if par == 0 else ((0, 2), (1, 0))
        for row_par in range(2):
            rows = ((0, 1),) if row_par == 0 else ((0, 2), (1, 0))
            total = None
            for plane, kd in depth:
                for start, kr in rows:
                    x = pad[plane, start : start + h2].reshape(cells, 128)
                    weights = jnp.concatenate(
                        [w1[kd, kr, 1], w1[kd, kr, 2], zeros, w1[kd, kr, 0]], axis=0
                    )
                    term = dot(x, weights, NT)
                    total = term if total is None else total + term
            both = total[:, 0:128] + roll_rows(total[:, 128:256], -1)
            turned = pltpu.roll(both, 64, 1)
            both = both.reshape(h2, PAD, 128)
            turned = turned.reshape(h2, PAD, 128)
            for r in range(h2):
                tmp[r % 2, pl.ds(0, w, 2), :] = both[r, 0:w]
                tmp[r % 2, pl.ds(1, w, 2), :] = turned[r, 0:w]
                out[par, 2 * r + row_par] = tmp[r % 2, :, 0:64].astype(BF16)


def input_backward(gp, upper, w1):
    return pl.pallas_call(
        input_kernel,
        out_shape=jax.ShapeDtypeStruct((2, 32, 48, 64), BF16),
        in_specs=vmem(3),
        out_specs=pl.BlockSpec(memory_space=pltpu.VMEM),
        scratch_shapes=[
            pltpu.VMEM((2, 17, PAD, 128), BF16),
            pltpu.VMEM((2, 48, 128), F32),
        ],
        name="input_backward",
        compiler_params=pltpu.CompilerParams(vmem_limit_bytes=10 << 20),
        cost_estimate=pl.CostEstimate(flops=1 << 30, bytes_accessed=2 << 20, transcendentals=0),
    )(gp, upper, w1)


def finish_kernel(scale, blocks, out):
    total = jnp.sum(blocks[...].astype(F32), axis=0) * scale
    packed = total[0:32]
    flipped = packed.T
    turned = jnp.concatenate([flipped[0:64], flipped[64:128]], axis=1)
    top = jnp.concatenate([turned[0:32], turned[32:64]], axis=1)
    mine = jnp.concatenate([top, total[32:48]], axis=0).astype(BF16)
    out[...] = jnp.broadcast_to(mine[None], out.shape)


def finish(blocks, count, scale):
    return pl.pallas_call(
        functools.partial(finish_kernel, scale),
        out_shape=jax.ShapeDtypeStruct((count, CHUNK, 128), BF16),
        in_specs=vmem(1),
        out_specs=pl.BlockSpec(memory_space=pltpu.VMEM),
        name="finish",
        compiler_params=pltpu.CompilerParams(vmem_limit_bytes=4 << 20),
        cost_estimate=pl.CostEstimate(flops=1 << 16, bytes_accessed=1 << 20, transcendentals=0),
    )(blocks)


def unpack_kernel(core, mine, other, first, second):
    first_core = core[0] == 0
    low = low_lanes((32, 128))
    for tap in range(mine.shape[0]):
        a = mine[tap].astype(F32)
        b = other[tap].astype(F32)
        half0 = jnp.where(first_core, a, b)
        half1 = jnp.where(first_core, b, a)
        top, bottom = half0[0:32], half1[0:32]
        first[tap, 0:32] = jnp.where(low, top, half_turn(bottom))
        first[tap, 32:64] = jnp.where(low, half_turn(top), bottom)
        second[tap, :, 0:128] = half0[32:48]
        second[tap, :, 128:256] = half1[32:48]


def unpack(core, mine, other):
    step = 9
    halves = pl.BlockSpec((step, CHUNK, 128), lambda i: (i, 0, 0))
    return pl.pallas_call(
        unpack_kernel,
        grid=(TAPS // step,),
        out_shape=(
            jax.ShapeDtypeStruct((TAPS, 64, 128), F32),
            jax.ShapeDtypeStruct((TAPS, 16, 256), F32),
        ),
        in_specs=[pl.BlockSpec(memory_space=pltpu.SMEM), halves, halves],
        out_specs=(
            pl.BlockSpec((step, 64, 128), lambda i: (i, 0, 0)),
            pl.BlockSpec((step, 16, 256), lambda i: (i, 0, 0)),
        ),
        name="unpack",
        compiler_params=pltpu.CompilerParams(vmem_limit_bytes=8 << 20),
        cost_estimate=pl.CostEstimate(flops=0, bytes_accessed=3 << 20, transcendentals=0),
    )(core, mine, other)


def exchange(blocks, axes):
    return lax.all_to_all(blocks, axes, split_axis=0, concat_axis=0, tiled=True)


def repeated(block, axes):
    return jnp.broadcast_to(block[None], (lax.axis_size(axes),) + block.shape)


def added(a, b):
    return (a.astype(F32) + b.astype(F32)).astype(BF16)


def total(blocks):
    return jnp.sum(blocks.astype(F32), axis=0)


def swap_cores(array):
    return lax.ppermute(array, "core", [(0, 1), (1, 0)])


def on_device(volume, cotangent, w_first, w_second):
    plane = ("z", "x")
    line = ("yl", "yh")
    core = lax.axis_index("core").astype(jnp.int32).reshape(1)
    cot = cotangent[0, 0]
    w2 = w_second.reshape(TAPS, 16, 256)
    packed = pack(pltpu.with_memory_space_constraint(volume, pltpu.HBM), cot)
    got = shifted(packed, 1)
    cot_after, _ = lax.optimization_barrier((cot, packed))
    cot_hi = shifted(cot_after, -1)
    pre, gh, even, odd, wd = early(volume, packed, cot, w_first, w2)
    gh, cpad_hi = upper_share(cot_hi, gh, wd)
    gp, keep, send = middle(core, got, cpad_hi, cot, pre, gh, even, odd, w_first, wd)
    upper = shifted(gp, -1)
    half = added(keep, swap_cores(send))
    parts, upper = lax.optimization_barrier((exchange(half, plane), upper))
    mine = total(parts).astype(BF16)
    blocks = exchange(repeated(mine, line), line)
    count = lax.axis_size(SAMPLE_AXES) * lax.axis_size(DEPTH_AXES) * 16 * 24
    scale = float(count) ** (-0.5)
    own_half = exchange(finish(blocks, lax.axis_size(plane), scale), plane)
    grad_input = input_backward(gp, upper, w_first)
    first, second = unpack(core, own_half, swap_cores(own_half))
    return (grad_input[None], first.reshape(3, 3, 3, 64, 128), second.reshape(3, 3, 3, 16, 256))


def solution(mesh):
    fine = Mesh(mesh.devices.reshape(2, 2, 8, 4, 4), SAMPLE_AXES + DEPTH_AXES)
    split = P(SAMPLE_AXES, DEPTH_AXES, None, None, None)
    return jax.shard_map(
        on_device,
        mesh=fine,
        in_specs=(split, split, P(), P()),
        out_specs=(split, P(), P()),
        check_vma=False,
    )
```

```python
import functools

import jax
import jax.numpy as jnp
from jax import lax
from jax.experimental import pallas as pl
from jax.experimental.pallas import tpu as pltpu
from jax.sharding import Mesh
from jax.sharding import PartitionSpec as P

GROUPS = 8
SAMPLE_AXES = ("yl", "core")
DEPTH_AXES = ("z", "x", "yh")
TAPS = 27
CHUNK = 48
PAD = 32
F32 = jnp.float32
BF16 = jnp.bfloat16

NT = (((1,), (1,)), ((), ()))
NN = (((1,), (0,)), ((), ()))
TN = (((0,), (0,)), ((), ()))


def dot(a, b, dims):
    return lax.dot_general(a, b, dims, preferred_element_type=F32)


def vmem(n):
    return [pl.BlockSpec(memory_space=pltpu.VMEM)] * n


def shifted(array, by):
    size = lax.axis_size(DEPTH_AXES)
    pairs = [(i, i + by) for i in range(size) if 0 <= i + by < size]
    return lax.ppermute(array, DEPTH_AXES, pairs)


def clear(ref):
    ref[...] = jnp.zeros_like(ref)


def roll_rows(x, by):
    return pltpu.roll(x, by % x.shape[0], 0)


def half_turn(x):
    return pltpu.roll(x, 64, x.ndim - 1)


def low_lanes(shape):
    return lax.broadcasted_iota(jnp.int32, shape, len(shape) - 1) < 64


def pair_rows(plane, out, tmp):
    step = tmp.shape[0]
    low = low_lanes((step, 24, 128))

    def body(i, carry):
        r = i * step
        tmp[:, :, 0:64] = plane[pl.ds(r, step)].astype(F32)
        even = tmp[:, pl.ds(0, 24, 2), :]
        odd = half_turn(tmp[:, pl.ds(1, 24, 2), :])
        out[pl.ds(r, step)] = jnp.where(low, even, odd).astype(BF16)
        return carry

    lax.fori_loop(0, plane.shape[0] // step, body, 0)


def pack_kernel(vol, cot, out, tmp):
    pair_rows(vol.at[0, 0], out.at[0, 0:8], tmp)
    out[0, 8:12] = cot[:, :, 0:128]
    out[0, 12:16] = cot[:, :, 128:256]


def pack(volume, cot):
    return pl.pallas_call(
        pack_kernel,
        grid=(4,),
        out_shape=jax.ShapeDtypeStruct((4, 16, 24, 128), BF16),
        in_specs=[
            pl.BlockSpec((1, 1, 8, 48, 64), lambda i: (0, 1, i, 0, 0)),
            pl.BlockSpec((4, 24, 256), lambda i: (i, 0, 0)),
        ],
        out_specs=pl.BlockSpec((1, 16, 24, 128), lambda i: (i, 0, 0, 0)),
        scratch_shapes=[pltpu.VMEM((8, 48, 128), F32)],
        name="pack",
        compiler_params=pltpu.CompilerParams(vmem_limit_bytes=4 << 20),
        cost_estimate=pl.CostEstimate(flops=0, bytes_accessed=2 << 20, transcendentals=0),
    )(volume, cot)


def split_rows(packed, even, odd):
    for r in range(16):
        even[r, 0:24] = packed[r // 4, 2 * (r % 4)]
        odd[r + 1, 0:24] = packed[r // 4, 2 * (r % 4) + 1]


def window(even, odd, kr):
    rows = even[...] if kr == 1 else odd[kr // 2 : kr // 2 + 16]
    return rows.reshape(16 * PAD, 128)


def strided_terms(windows, w1):
    zeros = jnp.zeros((64, 128), BF16)

    def weights(kd, kr):
        left = jnp.concatenate([w1[kd, kr, 1], w1[kd, kr, 2]], axis=0)
        right = jnp.concatenate([zeros, w1[kd, kr, 0]], axis=0)
        return jnp.concatenate([left, right], axis=1)

    total = None
    for i in range(0, len(windows), 2):
        pair = windows[i : i + 2]
        x = jnp.concatenate([p[2] for p in pair], axis=1) if len(pair) == 2 else pair[0][2]
        w = jnp.concatenate([weights(p[0], p[1]) for p in pair], axis=0)
        term = dot(x, w, NN)
        total = term if total is None else total + term
    return total[:, 0:128] + roll_rows(total[:, 128:256], 1)


def own_group():
    lane_group = lax.broadcasted_iota(jnp.int32, (128, 256), 1) // 32
    return lane_group == lax.broadcasted_iota(jnp.int32, (128, 256), 0) // 16


def put_weights(w2, kd, wd):
    own = own_group()
    for kr in range(3):
        for kc in range(3):
            spread = jnp.concatenate([w2[kd * 9 + kr * 3 + kc]] * GROUPS, axis=0)
            wd[kr, kc * 128 : kc * 128 + 128] = jnp.where(own, spread, 0.0).astype(BF16)


def cot_window(cpad, kr):
    return cpad[2 - kr : 18 - kr].reshape(16 * PAD, 256)


def grouped_terms(cpad, wd):
    total = None
    for kr in range(3):
        term = dot(cot_window(cpad, kr), wd[kr], NT)
        total = term if total is None else total + term
    return total


def join_columns(total):
    return roll_rows(total[:, 0:128], -1) + total[:, 128:256] + roll_rows(total[:, 256:384], 1)


def early_kernel(vol, packed, cot, w1, w2, pre, gh, even, odd, wd02, tmp, pairs, cpad, wd):
    clear(even)
    clear(odd)
    clear(cpad)
    for g in range(4):
        pair_rows(vol.at[0, 0, 8 * g : 8 * g + 8], pairs.at[g], tmp)
    split_rows(pairs, even.at[0], odd.at[0])
    split_rows(packed, even.at[1], odd.at[1])
    cpad[1:17, 0:24] = cot[...]
    windows = []
    for kd in (1, 2):
        for kr in range(3):
            windows.append((kd, kr, window(even.at[kd - 1], odd.at[kd - 1], kr)))
    pre[...] = strided_terms(windows, w1)
    put_weights(w2, 1, wd)
    gh[...] = join_columns(grouped_terms(cpad, wd))
    put_weights(w2, 0, wd02.at[0])
    put_weights(w2, 2, wd02.at[1])


def early(volume, packed, cot, w1, w2):
    whole = lambda *shape: pl.BlockSpec(shape, lambda i: (0,) * len(shape))
    return pl.pallas_call(
        early_kernel,
        grid=(1,),
        out_shape=(
            jax.ShapeDtypeStruct((16 * PAD, 128), F32),
            jax.ShapeDtypeStruct((16 * PAD, 128), F32),
            jax.ShapeDtypeStruct((2, 16, PAD, 128), BF16),
            jax.ShapeDtypeStruct((2, 17, PAD, 128), BF16),
            jax.ShapeDtypeStruct((2, 3, 384, 256), BF16),
        ),
        in_specs=[
            whole(1, 1, 32, 48, 64),
            whole(4, 16, 24, 128),
            whole(16, 24, 256),
            whole(3, 3, 3, 64, 128),
            whole(27, 16, 256),
        ],
        out_specs=(
            whole(16 * PAD, 128),
            whole(16 * PAD, 128),
            whole(2, 16, PAD, 128),
            whole(2, 17, PAD, 128),
            whole(2, 3, 384, 256),
        ),
        scratch_shapes=[
            pltpu.VMEM((8, 48, 128), F32),
            pltpu.VMEM((4, 8, 24, 128), BF16),
            pltpu.VMEM((18, PAD, 256), BF16),
            pltpu.VMEM((3, 384, 256), BF16),
        ],
        name="early",
        compiler_params=pltpu.CompilerParams(vmem_limit_bytes=12 << 20),
        cost_estimate=pl.CostEstimate(flops=1 << 30, bytes_accessed=2 << 20, transcendentals=0),
    )(volume, packed, cot, w1, w2)


def upper_kernel(cot_hi, gh_part, wd, gh, cpad):
    clear(cpad)
    cpad[1:17, 0:24] = cot_hi[...]
    gh[...] = gh_part[...] + join_columns(grouped_terms(cpad, wd.at[0]))


def upper_share(cot_hi, gh, wd):
    return pl.pallas_call(
        upper_kernel,
        out_shape=(
            jax.ShapeDtypeStruct((16 * PAD, 128), F32),
            jax.ShapeDtypeStruct((18, PAD, 256), BF16),
        ),
        in_specs=vmem(3),
        out_specs=tuple(vmem(2)),
        name="upper_share",
        compiler_params=pltpu.CompilerParams(vmem_limit_bytes=8 << 20),
        cost_estimate=pl.CostEstimate(flops=1 << 29, bytes_accessed=2 << 20, transcendentals=0),
    )(cot_hi, gh, wd)


def middle_kernel(
    core, got, cpad_hi, cot, pre_part, gh_part, even12, odd12, w1, wd,
    gp_out, keep_out, send_out,
    even0, odd0, cpad, hid, ups, hid_t, ups_t,
):
    cells = 16 * PAD
    clear(even0)
    clear(odd0)
    clear(cpad)
    cpad[1, 1:17, 0:24] = cot[...]
    split_rows(got, even0, odd0)
    for g in range(4):
        cpad[0, 1 + 4 * g : 5 + 4 * g, 0:24, 0:128] = got[g, 8:12]
        cpad[0, 1 + 4 * g : 5 + 4 * g, 0:24, 128:256] = got[g, 12:16]
    total = grouped_terms(cpad.at[0], wd.at[1])
    planes = (cpad_hi, cpad.at[1], cpad.at[0])
    gh = (join_columns(total) + gh_part[...]).astype(BF16).astype(F32)
    windows = [[window(even0, odd0, kr) for kr in range(3)]]
    for p in range(2):
        windows.append([window(even12.at[p], odd12.at[p], kr) for kr in range(3)])
    pre = strided_terms([(0, kr, windows[0][kr]) for kr in range(3)], w1) + pre_part[...]
    inside = (lax.broadcasted_iota(jnp.int32, (cells, 128), 0) & (PAD - 1)) < 24
    pre = jnp.where(inside, pre, 0.0)
    s = jax.nn.sigmoid(pre)
    hidden = (pre * s).astype(BF16).astype(F32)
    grad = gh * s * (1.0 + pre * (1.0 - s))
    grad = jnp.where(inside, grad, 0.0).astype(BF16).astype(F32)
    ups[:, 0:128] = grad.astype(BF16)
    ups[:, 128:256] = roll_rows(grad, -1).astype(BF16)
    hid[:, 0:128] = roll_rows(hidden, 1).astype(BF16)
    hid[:, 128:256] = hidden.astype(BF16)
    hid[:, 256:384] = roll_rows(hidden, -1).astype(BF16)
    gp_out[...] = ups[:, 0:128].reshape(16, PAD, 128)[:, 0:24]
    ups_t[...] = ups[...].T
    hid_t[...] = hid[...].T
    first_core = core[0] == 0

    def put(tap, row, half0, half1):
        size = half0.shape[0]
        keep_out[tap, row : row + size] = jnp.where(first_core, half0, half1).astype(BF16)
        send_out[tap, row : row + size] = jnp.where(first_core, half1, half0).astype(BF16)

    low = low_lanes((32, 128))
    flat = [windows[kd][kr] for kd in range(3) for kr in range(3)]
    for i in range(0, 9, 2):
        pair = flat[i : i + 2]
        x = jnp.concatenate(pair, axis=1) if len(pair) == 2 else pair[0]
        term = dot(ups_t[...], x, NN)
        for j in range(len(pair)):
            part = term[:, j * 128 : j * 128 + 128]
            tap = (i + j) * 3
            centre, side = [], []
            right = []
            for half in range(2):
                p = part[half * 64 : half * 64 + 32]
                q = part[half * 64 + 32 : half * 64 + 64]
                p1 = part[128 + half * 64 : 128 + half * 64 + 32]
                q1 = part[128 + half * 64 + 32 : 128 + half * 64 + 64]
                centre.append(jnp.where(low, p, half_turn(q)))
                right.append(jnp.where(low, half_turn(p), q))
                side.append(jnp.where(low, half_turn(p1), q1))
            put(tap, 0, *side)
            put(tap + 1, 0, *centre)
            put(tap + 2, 0, *right)
    own = own_group()
    for kd in range(3):
        for kr in range(3):
            term = dot(hid_t[...], cot_window(planes[kd], kr), NN)
            for kc in range(3):
                part = jnp.where(own, term[kc * 128 : kc * 128 + 128], 0.0)
                part = jnp.sum(part.reshape(GROUPS, 16, 256), axis=0)
                put((kd * 3 + kr) * 3 + kc, 32, part[:, 0:128], part[:, 128:256])


def middle(core, got, cpad_hi, cot, pre, gh, even, odd, w1, wd):
    return pl.pallas_call(
        middle_kernel,
        out_shape=(
            jax.ShapeDtypeStruct((16, 24, 128), BF16),
            jax.ShapeDtypeStruct((TAPS, CHUNK, 128), BF16),
            jax.ShapeDtypeStruct((TAPS, CHUNK, 128), BF16),
        ),
        in_specs=[pl.BlockSpec(memory_space=pltpu.SMEM)]
        + vmem(9),
        out_specs=tuple(vmem(3)),
        scratch_shapes=[
            pltpu.VMEM((16, PAD, 128), BF16),
            pltpu.VMEM((17, PAD, 128), BF16),
            pltpu.VMEM((2, 18, PAD, 256), BF16),
            pltpu.VMEM((16 * PAD, 384), BF16),
            pltpu.VMEM((16 * PAD, 256), BF16),
            pltpu.VMEM((384, 16 * PAD), BF16),
            pltpu.VMEM((256, 16 * PAD), BF16),
        ],
        name="middle",
        compiler_params=pltpu.CompilerParams(vmem_limit_bytes=20 << 20),
        cost_estimate=pl.CostEstimate(flops=3 << 30, bytes_accessed=4 << 20, transcendentals=1 << 16),
    )(core, got, cpad_hi, cot, pre, gh, even, odd, w1, wd)


def input_kernel(gp, upper, w1, out, pad, tmp):
    h2, w = gp.shape[0], gp.shape[1]
    cells = h2 * PAD
    clear(pad)
    pad[0, 0:h2, 0:w] = gp[...]
    pad[1, 0:h2, 0:w] = upper[...]
    zeros = jnp.zeros((64, 128), BF16)
    for par in range(2):
        depth = ((0, 1),) if par == 0 else ((0, 2), (1, 0))
        for row_par in range(2):
            rows = ((0, 1),) if row_par == 0 else ((0, 2), (1, 0))
            total = None
            for plane, kd in depth:
                for start, kr in rows:
                    x = pad[plane, start : start + h2].reshape(cells, 128)
                    weights = jnp.concatenate(
                        [w1[kd, kr, 1], w1[kd, kr, 2], zeros, w1[kd, kr, 0]], axis=0
                    )
                    term = dot(x, weights, NT)
                    total = term if total is None else total + term
            both = total[:, 0:128] + roll_rows(total[:, 128:256], -1)
            turned = pltpu.roll(both, 64, 1)
            both = both.reshape(h2, PAD, 128)
            turned = turned.reshape(h2, PAD, 128)
            for r in range(h2):
                tmp[r % 2, pl.ds(0, w, 2), :] = both[r, 0:w]
                tmp[r % 2, pl.ds(1, w, 2), :] = turned[r, 0:w]
                out[par, 2 * r + row_par] = tmp[r % 2, :, 0:64].astype(BF16)


def input_backward(gp, upper, w1):
    return pl.pallas_call(
        input_kernel,
        out_shape=jax.ShapeDtypeStruct((2, 32, 48, 64), BF16),
        in_specs=vmem(3),
        out_specs=pl.BlockSpec(memory_space=pltpu.VMEM),
        scratch_shapes=[
            pltpu.VMEM((2, 17, PAD, 128), BF16),
            pltpu.VMEM((2, 48, 128), F32),
        ],
        name="input_backward",
        compiler_params=pltpu.CompilerParams(vmem_limit_bytes=10 << 20),
        cost_estimate=pl.CostEstimate(flops=1 << 30, bytes_accessed=2 << 20, transcendentals=0),
    )(gp, upper, w1)


def finish_kernel(scale, blocks, out):
    total = jnp.sum(blocks[...].astype(F32), axis=0) * scale
    packed = total[0:32]
    flipped = packed.T
    turned = jnp.concatenate([flipped[0:64], flipped[64:128]], axis=1)
    top = jnp.concatenate([turned[0:32], turned[32:64]], axis=1)
    mine = jnp.concatenate([top, total[32:48]], axis=0).astype(BF16)
    out[...] = jnp.broadcast_to(mine[None], out.shape)


def finish(blocks, count, scale):
    return pl.pallas_call(
        functools.partial(finish_kernel, scale),
        out_shape=jax.ShapeDtypeStruct((count, CHUNK, 128), BF16),
        in_specs=vmem(1),
        out_specs=pl.BlockSpec(memory_space=pltpu.VMEM),
        name="finish",
        compiler_params=pltpu.CompilerParams(vmem_limit_bytes=4 << 20),
        cost_estimate=pl.CostEstimate(flops=1 << 16, bytes_accessed=1 << 20, transcendentals=0),
    )(blocks)


def unpack_kernel(core, mine, other, first, second):
    first_core = core[0] == 0
    low = low_lanes((32, 128))
    for tap in range(mine.shape[0]):
        a = mine[tap].astype(F32)
        b = other[tap].astype(F32)
        half0 = jnp.where(first_core, a, b)
        half1 = jnp.where(first_core, b, a)
        top, bottom = half0[0:32], half1[0:32]
        first[tap, 0:32] = jnp.where(low, top, half_turn(bottom))
        first[tap, 32:64] = jnp.where(low, half_turn(top), bottom)
        second[tap, :, 0:128] = half0[32:48]
        second[tap, :, 128:256] = half1[32:48]


def unpack(core, mine, other):
    step = 3
    halves = pl.BlockSpec((step, CHUNK, 128), lambda i: (i, 0, 0))
    return pl.pallas_call(
        unpack_kernel,
        grid=(TAPS // step,),
        out_shape=(
            jax.ShapeDtypeStruct((TAPS, 64, 128), F32),
            jax.ShapeDtypeStruct((TAPS, 16, 256), F32),
        ),
        in_specs=[pl.BlockSpec(memory_space=pltpu.SMEM), halves, halves],
        out_specs=(
            pl.BlockSpec((step, 64, 128), lambda i: (i, 0, 0)),
            pl.BlockSpec((step, 16, 256), lambda i: (i, 0, 0)),
        ),
        name="unpack",
        compiler_params=pltpu.CompilerParams(vmem_limit_bytes=8 << 20),
        cost_estimate=pl.CostEstimate(flops=0, bytes_accessed=3 << 20, transcendentals=0),
    )(core, mine, other)


def exchange(blocks, axes):
    return lax.all_to_all(blocks, axes, split_axis=0, concat_axis=0, tiled=True)


def repeated(block, axes):
    return jnp.broadcast_to(block[None], (lax.axis_size(axes),) + block.shape)


def added(a, b):
    return (a.astype(F32) + b.astype(F32)).astype(BF16)


def total(blocks):
    return jnp.sum(blocks.astype(F32), axis=0)


def swap_cores(array):
    return lax.ppermute(array, "core", [(0, 1), (1, 0)])


def on_device(volume, cotangent, w_first, w_second):
    plane = ("z", "x")
    line = ("yl", "yh")
    core = lax.axis_index("core").astype(jnp.int32).reshape(1)
    cot = cotangent[0, 0]
    w2 = w_second.reshape(TAPS, 16, 256)
    packed = pack(pltpu.with_memory_space_constraint(volume, pltpu.HBM), cot)
    got = shifted(packed, 1)
    cot_after, _ = lax.optimization_barrier((cot, packed))
    cot_hi = shifted(cot_after, -1)
    pre, gh, even, odd, wd = early(volume, packed, cot, w_first, w2)
    gh, cpad_hi = upper_share(cot_hi, gh, wd)
    gp, keep, send = middle(core, got, cpad_hi, cot, pre, gh, even, odd, w_first, wd)
    upper = shifted(gp, -1)
    spare = lax.axis_size(plane) - TAPS
    half = jnp.pad(added(keep, swap_cores(send)), ((0, spare), (0, 0), (0, 0)))
    parts, upper = lax.optimization_barrier((exchange(half, plane), upper))
    mine = total(parts).astype(BF16)
    blocks = exchange(repeated(mine, line), line)
    count = lax.axis_size(SAMPLE_AXES) * lax.axis_size(DEPTH_AXES) * 16 * 24
    scale = float(count) ** (-0.5)
    own_half = exchange(finish(blocks, lax.axis_size(plane), scale), plane)
    grad_input = input_backward(gp, upper, w_first)
    first, second = unpack(core, own_half, swap_cores(own_half))
    return (grad_input[None], first.reshape(3, 3, 3, 64, 128), second.reshape(3, 3, 3, 16, 256))


def solution(mesh):
    fine = Mesh(mesh.devices.reshape(2, 2, 8, 4, 4), SAMPLE_AXES + DEPTH_AXES)
    split = P(SAMPLE_AXES, DEPTH_AXES, None, None, None)
    return jax.shard_map(
        on_device,
        mesh=fine,
        in_specs=(split, split, P(), P()),
        out_specs=(split, P(), P()),
        check_vma=False,
    )
```
